128 devices in a mesh: group: 8 (over y, core), inner: 16 (over x, z).
Axes of the slice: x: 4, y: 4, z: 4, core: 2. Of those that a mesh axis runs over, the one named last changes fastest.
Arguments:
- grad_out: bfloat16 [16384, 2048], P(('group', 'inner')), may hold values from -4 to 4
- hidden_in: bfloat16 [16384, 2048], P(('group', 'inner')), may hold values from -6 to 6
- norm_gain: float32 [2048], replicated, may hold values from 0.5 to 1.5
- expert_ids: int32 [16384, 8], P(('group', 'inner')), may hold values from 0 to 127, all different within a row; in each aligned block of 128 rows (0 to 127, 128 to 255, ...) at most 10 rows name the same one
- gate_weights: float32 [16384, 8], P(('group', 'inner')), may hold values from 0.02 to 0.5
- gate_proj: bfloat16 [128, 2048, 768], P(('group', 'inner')), may hold values from -0.125 to 0.125
- up_proj: bfloat16 [128, 2048, 768], P(('group', 'inner')), may hold values from -0.125 to 0.125
- down_proj: bfloat16 [128, 768, 2048], P(('group', 'inner')), may hold values from -0.21875 to 0.21875
- out_proj: bfloat16 [4096, 2048], P('inner'), may hold values from -0.09375 to 0.09375
- query_rows: bfloat16 [16384, 4096], P('group', 'inner'), may hold values from -140 to 140
- key_rows: bfloat16 [16384, 4096], P('group', 'inner'), may hold values from -7 to 7
- value_rows: bfloat16 [16384, 4096], P('group', 'inner'), may hold values from -6 to 6
Outputs:
- grad_hidden: bfloat16 [16384, 2048], P(('group', 'inner'))
- grad_gate: bfloat16 [16384, 8], P(('group', 'inner'))
- grad_queries: bfloat16 [16384, 4096], P('group', 'inner')
- grad_keys: bfloat16 [16384, 4096], P('group', 'inner')
- grad_values: bfloat16 [16384, 4096], P('group', 'inner')
The draws below stay inside these ranges and needn't reach their ends.
Inputs may be any that keep to these rules, and one draw needn't show every extreme that they name: `expert_ids`: each row names 8 different experts; in the rows of one device no expert is named more than 10 times, a bound that some block reaches.
All inputs are finite; a program needn't handle non-finite values.
Results may differ from the reference program's by a relative error of at most 0.019.
Values may be sent and summed in bfloat16 or wider, within the bound.
No kernel may reach another device: no remote copies, remote signals or barrier semaphores. Data moves between devices by JAX's collectives and lax.ppermute only.
A program may use at most 128 MiB of HBM per device.

```python
import math
import jax
import jax.numpy as jnp
import numpy as np
from jax import lax

D = 2048
FF = 768
HEADS = 32
HD = 128
TOP = 8
TOK_DEV = 128
EXPERTS = 128
CAP = 10
TOKENS = 16384
LEN = 1024
N_GROUP = 8
N_INNER = 16


def joint_draw(key):
    base = jax.random.fold_in(key, 7123)
    first, second = jax.random.split(base, 2)
    shape = (TOKENS, HEADS, HD)
    key_vals = jax.random.truncated_normal(first, -6.0, 6.0, shape, jnp.float32)
    query_vals = jax.random.truncated_normal(second, -6.0, 6.0, shape, jnp.float32)
    return (query_vals.reshape(TOKENS, HEADS * HD), key_vals.reshape(TOKENS, HEADS * HD))


def draw_query_rows(key, part):
    return joint_draw(key)[0].astype(jnp.bfloat16)


def draw_key_rows(key, part):
    return joint_draw(key)[1].astype(jnp.bfloat16)


def block_levels(own_key, extent, shards, least, largest):
    gain = 1.0
    for dim, blocks in shards:
        steps = jax.random.uniform(jax.random.fold_in(jax.random.fold_in(own_key, 6), dim), (blocks,), jnp.float32, least / len(shards), largest / len(shards))
        gain = gain * jnp.repeat(jnp.exp(steps), extent[dim] // blocks).reshape((-1,) + (1,) * (len(extent) - 1 - dim))
    return gain


def deal_out(rng, own, number, rows, number_of, top, reach, lean):
    order = jax.random.permutation(rng, number_of)
    heavy_load, usual = portions_of(number_of, rows * top, reach, lean, True), portions_of(number_of, rows * top, reach, lean, False)
    places = jnp.arange(number_of)

    def named(lengths, offset_by):
        used = int((lengths > 0).sum())
        fixed = max(1, used // 4)
        shifted = fixed + (places - fixed + offset_by * (used - fixed)) % max(1, number_of - fixed)
        return jnp.zeros((number_of,), jnp.int32).at[order[jnp.where(places < fixed, places, shifted)]].set(jnp.asarray(lengths, jnp.int32))

    lengths = jnp.where(number % 4 == 0, named(heavy_load, number // 4), named(usual, number - number // 4 - 1))
    mixed = jax.random.permutation(jax.random.fold_in(own, 3), number_of)
    source_of, receiver = mixed[0:number_of // 2 * 2:2], mixed[1:number_of // 2 * 2:2]
    margin = jnp.minimum(lengths[source_of] - 1, reach - lengths[receiver]) // 2
    margin = jnp.where((source_of == order[0]) | (receiver == order[0]) | (lengths[receiver] == 0), 0, jnp.maximum(margin, 0))
    shifted = jax.random.randint(jax.random.fold_in(own, 4), (number_of // 2,), 0, 1 << 20) % (margin + 1)
    lengths = lengths.at[source_of].add(-shifted).at[receiver].add(shifted)
    members = jnp.searchsorted(jnp.cumsum(lengths), jnp.arange(rows * top), side="right").astype(jnp.int32)
    listing = members.reshape(top, rows).T
    listing = listing[jax.random.permutation(jax.random.fold_in(own, 1), rows)]
    offset_by = jax.random.randint(jax.random.fold_in(own, 2), (rows, 1), 0, top)
    return jnp.take_along_axis(listing, (jnp.arange(top)[None, :] + offset_by) % top, axis=1)


def portions_of(count, total, reach, skew, full):
    weights = [(1 << 20) // math.isqrt(standing ** skew) + 1 for standing in range(1, count + 1)]
    largest = reach if full else min(reach, max(-(-total // count), total * weights[0] // sum(weights)))
    least = 1 if total - largest >= count - 1 else 0
    holding, rest = [largest] + [least] * (count - 1), total - largest - least * (count - 1)
    while rest > 0:
        movable = [i for i in range(1, count) if holding[i] < largest] or [i for i in range(1, count) if holding[i] < reach]
        pool, remaining = sum([weights[i] for i in movable]), rest
        for i in movable:
            more = min(reach - holding[i], max(1, remaining * weights[i] // pool), rest)
            holding[i] = holding[i] + more
            rest = rest - more
    return np.array(holding)


def normal_values(rng, shape, deviation, reach, pieces=(), held_as=jnp.bfloat16):
    entries = jax.random.normal(rng, shape, jnp.float32) * deviation
    if len(pieces) > 0:
        entries = block_levels(rng, shape, pieces, -0.22, 0.18) * entries
    return jnp.clip(entries, min=-reach, max=reach).astype(held_as)


def setup_inputs(seed: int = 0) -> dict:
    key_list = jax.random.split(jax.random.key(seed), 13)
    grad_out = normal_values(key_list[0], (TOKENS, D), 0.5, 4.0, ((0, 128),))
    hidden_in = normal_values(key_list[1], (TOKENS, D), 1.0, 6.0, ((0, 128),))
    norm_gain = jnp.clip(1.0 + 0.1 * jax.random.normal(key_list[2], (D,), jnp.float32), 0.5, 1.5)
    expert_ids_keys = jax.random.split(jax.random.fold_in(key_list[3], 1), TOKENS // TOK_DEV)
    expert_ids_turns = jax.random.permutation(jax.random.fold_in(key_list[3], 3), TOKENS // TOK_DEV)
    expert_ids = jax.vmap(lambda own, number: deal_out(jax.random.fold_in(key_list[3], 2), own, number, TOK_DEV, EXPERTS, TOP, CAP, 2))(expert_ids_keys, expert_ids_turns).reshape((TOKENS, TOP))
    gate_weights = jnp.clip(jnp.exp(math.log(0.5) - 3.218876 * jax.random.uniform(key_list[4], (TOKENS, TOP), jnp.float32) ** block_levels(key_list[4], (TOKENS, TOP), ((0, 128),), -0.2, 0.2)), 0.02, 0.5)
    gate_proj = normal_values(key_list[5], (EXPERTS, D, FF), D ** -0.5, 0.125, ((0, 128),))
    up_proj = normal_values(key_list[6], (EXPERTS, D, FF), D ** -0.5, 0.125, ((0, 128),))
    down_proj = normal_values(key_list[7], (EXPERTS, FF, D), FF ** -0.5, 0.21875, ((0, 128),))
    out_proj = normal_values(key_list[8], (HEADS * HD, D), (HEADS * HD) ** -0.5, 0.09375, ((0, 16),))
    query_rows = draw_query_rows(jax.random.fold_in(key_list[12], 71), 0)
    key_rows = draw_key_rows(jax.random.fold_in(key_list[12], 71), 0)
    value_rows = normal_values(key_list[11], (TOKENS, HEADS * HD), 1.0, 6.0, ((0, 8), (1, 16)))
    return dict(grad_out=grad_out, hidden_in=hidden_in, norm_gain=norm_gain, expert_ids=expert_ids, gate_weights=gate_weights, gate_proj=gate_proj, up_proj=up_proj, down_proj=down_proj, out_proj=out_proj, query_rows=query_rows, key_rows=key_rows, value_rows=value_rows)


def dot_rt(left, right):
    return lax.dot_general(left, right, (((1,), (1,)), ((), ())), preferred_element_type=jnp.float32)

def expert_backward(grad_in, normed_in, gate_mat, up_mat, down_mat):
    gate_pre = jnp.dot(normed_in, gate_mat, preferred_element_type=jnp.float32)
    up_pre = jnp.dot(normed_in, up_mat, preferred_element_type=jnp.float32)
    sigma = jax.nn.sigmoid(gate_pre)
    act = gate_pre * sigma
    slope = sigma * (1.0 + gate_pre * (1.0 - sigma))
    expert_hidden = act * up_pre
    grad_hid = dot_rt(grad_in, down_mat)
    gate_score = lax.optimization_barrier(jnp.sum(grad_hid * expert_hidden, axis=1)).astype(jnp.bfloat16)
    grad_gatepre = (grad_hid * up_pre * slope).astype(jnp.bfloat16)
    grad_uppre = (grad_hid * act).astype(jnp.bfloat16)
    pair_grad = (dot_rt(grad_gatepre, gate_mat) + dot_rt(grad_uppre, up_mat)).astype(jnp.bfloat16)
    return (pair_grad, gate_score)

def attention_grads(grad_attn, query_rows, key_rows, value_rows):
    seq_count = query_rows.shape[0] // LEN

    def by_head(matrix):
        return matrix.reshape(seq_count, LEN, HEADS, HD).transpose(2, 0, 1, 3).astype(jnp.float32)
    att_scale = HD ** (-0.5)
    causal = jnp.arange(LEN)[:, None] >= jnp.arange(LEN)[None, :]

    def one_head(block_item):
        query, key_part, value, grad_part = block_item
        scores = jnp.einsum('sqd,skd->sqk', query, key_part) * att_scale
        scores = jnp.where(causal[None], scores, -jnp.inf)
        peak = lax.optimization_barrier(jnp.max(scores, axis=2, keepdims=True))
        exp_scores = jnp.exp(scores - peak)
        probs = exp_scores / lax.optimization_barrier(jnp.sum(exp_scores, axis=2, keepdims=True))
        probs_half = lax.optimization_barrier(probs.astype(jnp.bfloat16)).astype(jnp.float32)
        grad_v = jnp.einsum('sqk,sqd->skd', probs_half, grad_part).astype(jnp.bfloat16)
        grad_probs = jnp.einsum('sqd,skd->sqk', grad_part, value)
        delta = lax.optimization_barrier(jnp.sum(probs * grad_probs, axis=2, keepdims=True))
        grad_scores = lax.optimization_barrier((probs * (grad_probs - delta)).astype(jnp.bfloat16)).astype(jnp.float32)
        grad_q = (att_scale * jnp.einsum('sqk,skd->sqd', grad_scores, key_part)).astype(jnp.bfloat16)
        grad_k = (att_scale * jnp.einsum('sqk,sqd->skd', grad_scores, query)).astype(jnp.bfloat16)
        return (grad_q, grad_k, grad_v)
    stacked = lax.map(one_head, (by_head(query_rows), by_head(key_rows), by_head(value_rows), by_head(grad_attn)))

    def by_token(result):
        return result.transpose(1, 2, 0, 3).reshape(seq_count * LEN, HEADS * HD)
    return (by_token(stacked[0]), by_token(stacked[1]), by_token(stacked[2]))

def reference(grad_out, hidden_in, norm_gain, expert_ids, gate_weights, gate_proj, up_proj, down_proj, out_proj, query_rows, key_rows, value_rows):
    token_count, model_width = grad_out.shape
    hid_full = hidden_in.astype(jnp.float32)
    inv_rms = lax.rsqrt(lax.optimization_barrier(jnp.mean(hid_full * hid_full, axis=1, keepdims=True)) + 1e-06)
    normal_rows = hid_full * inv_rms
    normed = (normal_rows * norm_gain).astype(jnp.bfloat16)
    flat_ids = expert_ids.reshape(-1).astype(jnp.int32)
    pair_count = flat_ids.shape[0]
    flat_gates = gate_weights.reshape(-1)
    order = jnp.argsort(flat_ids, stable=True).astype(jnp.int32)
    counts = jnp.bincount(flat_ids, length=EXPERTS).astype(jnp.int32)
    starts = (jnp.cumsum(counts) - counts).astype(jnp.int32)
    bound = N_GROUP * N_INNER * CAP

    def per_expert(carry, expert):
        moe_grad, gate_grad = carry
        position = starts[expert] + jnp.arange(bound, dtype=jnp.int32)
        valid = jnp.arange(bound, dtype=jnp.int32) < counts[expert]
        pair_index = order[jnp.minimum(position, pair_count - 1)].astype(jnp.int32)
        token_index = (pair_index // TOP).astype(jnp.int32)
        pair_grad, gate_score = expert_backward(grad_out[token_index], normed[token_index], gate_proj[expert], up_proj[expert], down_proj[expert])
        weight = jnp.where(valid, flat_gates[pair_index], 0.0)
        pair_full = lax.optimization_barrier(pair_grad).astype(jnp.float32)
        moe_grad = moe_grad.at[token_index].add(weight[:, None] * pair_full)
        score_full = lax.optimization_barrier(gate_score).astype(jnp.float32)
        gate_grad = gate_grad.at[pair_index].add(jnp.where(valid, score_full, 0.0))
        return ((moe_grad, gate_grad), None)
    start_carry = (jnp.zeros((token_count, model_width), jnp.float32), jnp.zeros((pair_count,), jnp.float32))
    (moe_grad, gate_grad), unused = lax.scan(per_expert, start_carry, jnp.arange(EXPERTS, dtype=jnp.int32))
    grad_gate = gate_grad.reshape(token_count, TOP).astype(jnp.bfloat16)
    scaled = moe_grad * norm_gain
    inner_mean = lax.optimization_barrier(jnp.mean(scaled * normal_rows, axis=1, keepdims=True))
    grad_hidden = (grad_out.astype(jnp.float32) + inv_rms * (scaled - normal_rows * inner_mean)).astype(jnp.bfloat16)
    grad_attn = dot_rt(grad_hidden, out_proj).astype(jnp.bfloat16)
    grad_queries, grad_keys, grad_values = attention_grads(grad_attn, query_rows, key_rows, value_rows)
    return (grad_hidden, grad_gate, grad_queries, grad_keys, grad_values)
```

```python
import functools

import jax
import jax.numpy as jnp
from jax import lax
from jax.experimental import pallas as pl
from jax.experimental.pallas import tpu as pltpu
from jax.sharding import PartitionSpec as P

HD = 128
SEQS = 2
SLOTS = 8
EXTRA = 2
PARTS = 4
LANES = 128
BF = jnp.bfloat16
F32 = jnp.float32


def dot_nn(left, right):
    return lax.dot_general(left, right, (((1,), (0,)), ((), ())), preferred_element_type=F32)


def dot_nt(left, right):
    return lax.dot_general(left, right, (((1,), (1,)), ((), ())), preferred_element_type=F32)


def dot_tn(left, right):
    return lax.dot_general(left, right, (((0,), (0,)), ((), ())), preferred_element_type=F32)


def iota(shape, dim):
    return lax.broadcasted_iota(jnp.int32, shape, dim)


def routing(ids, experts):
    tokens, top = ids.shape
    lane = iota((tokens, experts), 1)
    member = jnp.zeros((tokens, experts), F32)
    for k in range(top):
        member = member + jnp.where(ids[:, k : k + 1] == lane, 1.0, 0.0)
    earlier = jnp.where(iota((tokens, tokens), 1) < iota((tokens, tokens), 0), 1.0, 0.0).astype(BF)
    slot = dot_nn(earlier, member.astype(BF))
    return jnp.where(member > 0.5, slot, -1.0)


def per_row(by_expert):
    experts, width = by_expert.shape
    return jnp.broadcast_to(by_expert[:, None, :], (experts, SLOTS, width)).reshape(
        experts * SLOTS, width
    )


def dispatch_kernel(ids_ref, grad_ref, hid_ref, gain_ref, out_ref, rows_ref, parts_ref, slot_ref):
    tokens, width = grad_ref.shape
    experts = slot_ref.shape[0]
    step = pl.program_id(0)
    block_experts = out_ref.shape[0] // SLOTS
    piece = 2 * width // PARTS

    @pl.when(step == 0)
    def _():
        hid = hid_ref[...].astype(F32)
        inv_rms = lax.rsqrt(jnp.mean(hid * hid, axis=1, keepdims=True) + 1e-06)
        normed = (hid * inv_rms * gain_ref[...]).astype(BF)
        grad = grad_ref[...]
        rows_ref[:, :width] = grad
        rows_ref[:, width:] = normed
        half = PARTS // 2
        for part in range(half):
            parts_ref[part * tokens : (part + 1) * tokens, :] = grad[
                :, part * piece : (part + 1) * piece
            ]
            parts_ref[(half + part) * tokens : (half + part + 1) * tokens, :] = normed[
                :, part * piece : (part + 1) * piece
            ]
        slot_ref[...] = routing(ids_ref[...], experts).T

    start = pl.multiple_of(step * block_experts, block_experts)
    slot = per_row(slot_ref[pl.ds(start, block_experts), :])
    place = iota(slot.shape, 0) & (SLOTS - 1)
    pick = jnp.where(slot == place.astype(F32), 1.0, 0.0).astype(BF)
    chunk = 1024
    for col in range(0, 2 * width, chunk):
        out_ref[:, col : col + chunk] = dot_nn(pick, rows_ref[:, col : col + chunk]).astype(BF)
    late = slot == (SLOTS + (place >> 2)).astype(F32)
    pick_late = jnp.concatenate(
        [
            jnp.where(late & ((place & (PARTS - 1)) == part), 1.0, 0.0).astype(BF)
            for part in range(PARTS)
        ],
        axis=1,
    )
    out_ref[:, 2 * width :] = dot_nn(pick_late, parts_ref[...]).astype(BF)


def dispatch(ids, grad_out, hidden_in, gain, experts):
    tokens, width = grad_out.shape
    total = 2 * width + 2 * width // PARTS
    steps = 4
    rows = experts * SLOTS
    whole = lambda shape: pl.BlockSpec(shape, lambda i: (0,) * len(shape))
    return pl.pallas_call(
        dispatch_kernel,
        out_shape=jax.ShapeDtypeStruct((rows, total), BF),
        grid=(steps,),
        in_specs=[
            whole(ids.shape),
            whole(grad_out.shape),
            whole(hidden_in.shape),
            whole(gain.shape),
        ],
        out_specs=pl.BlockSpec((rows // steps, total), lambda i: (i, 0)),
        scratch_shapes=[
            pltpu.VMEM((tokens, 2 * width), BF),
            pltpu.VMEM((PARTS * tokens, 2 * width // PARTS), BF),
            pltpu.VMEM((experts, tokens), F32),
        ],
        compiler_params=pltpu.CompilerParams(vmem_limit_bytes=32 << 20),
        name="dispatch",
    )(ids, grad_out, hidden_in, gain)


def expert_kernel(rows_ref, gate_ref, up_ref, down_ref, out_ref, grad_ref, norm_ref):
    width = gate_ref.shape[0]
    main = rows_ref.shape[0]
    late = main // SLOTS * EXTRA
    half = width // 2
    grad_ref[:main, :] = rows_ref[:, :width]
    norm_ref[:main, :] = rows_ref[:, width : 2 * width]
    order = iota((main, main), 0)
    source = (order % late) * PARTS + order // late
    gather = jnp.where(iota((main, main), 1) == source, 1.0, 0.0).astype(BF)
    moved = dot_nn(gather, rows_ref[:, 2 * width :]).astype(BF)
    for part in range(2):
        cols = slice(part * half, (part + 1) * half)
        grad_ref[main:, cols] = moved[part * late : (part + 1) * late]
        norm_ref[main:, cols] = moved[(2 + part) * late : (3 + part) * late]
    norm = norm_ref[...]
    gate_pre = dot_nn(norm, gate_ref[...])
    up_pre = dot_nn(norm, up_ref[...])
    sigma = jax.nn.sigmoid(gate_pre)
    act = gate_pre * sigma
    slope = sigma * (1.0 + gate_pre * (1.0 - sigma))
    grad_hid = dot_nt(grad_ref[...], down_ref[...])
    grad_uppre = grad_hid * act
    score = jnp.sum(grad_uppre * up_pre, axis=1, keepdims=True)
    grad_gatepre = (grad_hid * up_pre * slope).astype(BF)
    grad_uppre = grad_uppre.astype(BF)
    pair = (dot_nt(grad_gatepre, gate_ref[...]) + dot_nt(grad_uppre, up_ref[...])).astype(BF)
    out_ref[:, :width] = pair[:main]
    quarter = width // PARTS
    stacked = jnp.concatenate(
        [pair[main:, part * quarter : (part + 1) * quarter] for part in range(PARTS)], axis=0
    )
    order = iota((main, main), 1)
    scatter = jnp.where(
        iota((main, main), 0) == (order % late) * PARTS + order // late, 1.0, 0.0
    ).astype(BF)
    out_ref[:, width : width + quarter] = dot_nn(scatter, stacked).astype(BF)
    spread = jnp.where((iota((main, late), 0) >> 2) == iota((main, late), 1), 1.0, 0.0).astype(BF)
    late_score = dot_nn(spread, jnp.broadcast_to(score[main:], (late, LANES)).astype(BF))
    lane = iota((main, LANES), 1)
    out_ref[:, width + quarter :] = jnp.where(
        lane == 0, score[:main], jnp.where(lane == 1, late_score, 0.0)
    ).astype(BF)


def expert_backward(arrived, gate_mat, up_mat, down_mat):
    rows, total = arrived.shape
    width, hidden = gate_mat.shape
    steps = 2
    main = rows // steps
    both = main + main // SLOTS * EXTRA
    out_width = width + width // PARTS + LANES
    fixed = lambda shape: pl.BlockSpec(
        shape, lambda i: (0,) * len(shape), pipeline_mode=pl.Buffered(1)
    )
    return pl.pallas_call(
        expert_kernel,
        out_shape=jax.ShapeDtypeStruct((rows, out_width), BF),
        grid=(steps,),
        in_specs=[
            pl.BlockSpec((main, total), lambda i: (i, 0)),
            fixed(gate_mat.shape),
            fixed(up_mat.shape),
            fixed(down_mat.shape),
        ],
        out_specs=pl.BlockSpec((main, out_width), lambda i: (i, 0)),
        scratch_shapes=[pltpu.VMEM((both, width), BF), pltpu.VMEM((both, width), BF)],
        compiler_params=pltpu.CompilerParams(vmem_limit_bytes=56 << 20),
        name="expert",
    )(arrived, gate_mat, up_mat, down_mat)


def combine_kernel(ids_ref, weight_ref, grad_ref, hid_ref, gain_ref, back_ref, out_ref, gate_ref):
    tokens, width = grad_ref.shape
    rows = back_ref.shape[0]
    experts = rows // SLOTS
    quarter = width // PARTS
    ids = ids_ref[...]
    weights = weight_ref[...]
    top = ids.shape[1]
    lane = iota((tokens, experts), 1)
    weight = jnp.zeros((tokens, experts), F32)
    for k in range(top):
        weight = weight + jnp.where(ids[:, k : k + 1] == lane, weights[:, k : k + 1], 0.0)
    slot = per_row(routing(ids, experts).T)
    weight = per_row(weight.T)
    place = iota(slot.shape, 0) & (SLOTS - 1)
    first = slot == place.astype(F32)
    late = slot == (SLOTS + (place >> 2)).astype(F32)
    high = weight.astype(BF).astype(F32)
    low = weight - high
    pick = jnp.concatenate(
        [jnp.where(first, high, 0.0).astype(BF), jnp.where(first, low, 0.0).astype(BF)], axis=1
    )
    moe = dot_tn(pick, back_ref[:, :width])
    moe = moe[:tokens] + moe[tokens:]
    pick_late = jnp.concatenate(
        [
            jnp.where(late & ((place & (PARTS - 1)) == part), value, 0.0).astype(BF)
            for part in range(PARTS)
            for value in (high, low)
        ],
        axis=1,
    )
    moe_late = dot_tn(pick_late, back_ref[:, width : width + quarter])
    moe_late = jnp.concatenate(
        [
            moe_late[2 * part * tokens : (2 * part + 1) * tokens]
            + moe_late[(2 * part + 1) * tokens : (2 * part + 2) * tokens]
            for part in range(PARTS)
        ],
        axis=1,
    )
    moe = moe + moe_late
    hid = hid_ref[...].astype(F32)
    inv_rms = lax.rsqrt(jnp.mean(hid * hid, axis=1, keepdims=True) + 1e-06)
    normal = hid * inv_rms
    scaled = moe * gain_ref[...]
    inner_mean = jnp.mean(scaled * normal, axis=1, keepdims=True)
    out_ref[...] = (grad_ref[...].astype(F32) + inv_rms * (scaled - normal * inner_mean)).astype(BF)
    score = back_ref[:, width + quarter :].astype(F32)
    got = jnp.where(first, score[:, 0:1], 0.0) + jnp.where(
        late & ((place & (PARTS - 1)) == 0), score[:, 1:2], 0.0
    )
    by_expert = jnp.sum(got.reshape(experts, SLOTS, tokens), axis=1).T
    column = iota((tokens, top), 1)
    gate = jnp.zeros((tokens, top), F32)
    for k in range(top):
        value = jnp.sum(jnp.where(ids[:, k : k + 1] == lane, by_expert, 0.0), axis=1, keepdims=True)
        gate = gate + jnp.where(column == k, value, 0.0)
    gate_ref[...] = gate.astype(BF)


def combine(ids, weights, grad_out, hidden_in, gain, back):
    return pl.pallas_call(
        combine_kernel,
        out_shape=(
            jax.ShapeDtypeStruct(grad_out.shape, BF),
            jax.ShapeDtypeStruct(ids.shape, BF),
        ),
        compiler_params=pltpu.CompilerParams(vmem_limit_bytes=48 << 20),
        name="combine",
    )(ids, weights, grad_out, hidden_in, gain, back)


def attention_kernel(hidden_ref, proj_ref, q_ref, k_ref, v_ref, dq_ref, dk_ref, dv_ref, acc_k, acc_v):
    length = q_ref.shape[0]
    scale = HD ** (-0.5)
    block = 256
    grad_all = dot_nt(hidden_ref[...], proj_ref[...]).astype(BF)
    for i in range(length // block):
        lo, hi = i * block, (i + 1) * block
        query = q_ref[lo:hi, :]
        grad = grad_all[lo:hi]
        keys = k_ref[:hi, :]
        scores = dot_nt(keys, query)
        corner = jnp.where(
            iota((block, block), 0) <= iota((block, block), 1), scores[lo:hi], -jnp.inf
        )
        scores = jnp.concatenate([scores[:lo], corner], axis=0) if i else corner
        peak = jnp.max(scores, axis=0, keepdims=True)
        exp_scores = jnp.exp((scores - peak) * scale)
        probs = exp_scores * (1.0 / jnp.sum(exp_scores, axis=0, keepdims=True))
        grad_probs = dot_nt(v_ref[:hi, :], grad)
        delta = jnp.sum(probs * grad_probs, axis=0, keepdims=True)
        grad_scores = (probs * (grad_probs - delta)).astype(BF)
        dq_ref[lo:hi, :] = (scale * dot_tn(grad_scores, keys)).astype(BF)
        dv = dot_nn(probs.astype(BF), grad)
        dk = dot_nn(grad_scores, query)
        if i:
            acc_k[:lo, :] += dk[:lo]
            acc_v[:lo, :] += dv[:lo]
        acc_k[lo:hi, :] = dk[lo:]
        acc_v[lo:hi, :] = dv[lo:]
    dk_ref[...] = (scale * acc_k[...]).astype(BF)
    dv_ref[...] = acc_v[...].astype(BF)


def attention(hidden, proj, query, key, value):
    tokens, cols = query.shape
    length = tokens // SEQS
    width = hidden.shape[1]
    item = pl.BlockSpec((length, HD), lambda s, h: (s, h))
    return pl.pallas_call(
        attention_kernel,
        out_shape=[jax.ShapeDtypeStruct(query.shape, BF)] * 3,
        grid=(SEQS, cols // HD),
        in_specs=[
            pl.BlockSpec((length, width), lambda s, h: (s, 0)),
            pl.BlockSpec((HD, width), lambda s, h: (h, 0)),
            item,
            item,
            item,
        ],
        out_specs=[item] * 3,
        scratch_shapes=[pltpu.VMEM((length, HD), F32), pltpu.VMEM((length, HD), F32)],
        compiler_params=pltpu.CompilerParams(vmem_limit_bytes=48 << 20),
        name="attention",
    )(hidden, proj, query, key, value)


def exchange(rows, experts):
    total = rows.shape[1]
    moved = lax.all_to_all(
        rows.reshape(experts, SLOTS, total),
        ("group", "inner"),
        split_axis=0,
        concat_axis=0,
        tiled=True,
    )
    return moved.reshape(experts * SLOTS, total)


def local(
    grad_out,
    hidden_in,
    norm_gain,
    expert_ids,
    gate_weights,
    gate_proj,
    up_proj,
    down_proj,
    out_proj,
    query_rows,
    key_rows,
    value_rows,
):
    experts = lax.axis_size("group") * lax.axis_size("inner")
    gain = norm_gain.reshape(1, -1)
    outgoing = dispatch(expert_ids, grad_out, hidden_in, gain, experts)
    arrived = exchange(outgoing, experts)
    answers = expert_backward(arrived, gate_proj[0], up_proj[0], down_proj[0])
    back = exchange(answers, experts)
    grad_hidden, grad_gate = combine(
        expert_ids, gate_weights, grad_out, hidden_in, gain, back
    )
    gathered = lax.all_gather(grad_hidden, "inner", axis=0, tiled=True)
    grad_q, grad_k, grad_v = attention(gathered, out_proj, query_rows, key_rows, value_rows)
    return (grad_hidden, grad_gate, grad_q, grad_k, grad_v)


def solution(mesh):
    rows = P(("group", "inner"), None)
    stack = P(("group", "inner"), None, None)
    heads = P("group", "inner")
    return jax.shard_map(
        local,
        mesh=mesh,
        in_specs=(
            rows,
            rows,
            P(),
            rows,
            rows,
            stack,
            stack,
            stack,
            P("inner", None),
            heads,
            heads,
            heads,
        ),
        out_specs=(rows, rows, heads, heads, heads),
        check_vma=False,
    )
```

```python
import functools

import jax
import jax.numpy as jnp
from jax import lax
from jax.experimental import pallas as pl
from jax.experimental.pallas import tpu as pltpu
from jax.sharding import PartitionSpec as P

HD = 128
SEQS = 2
SLOTS = 8
EXTRA = 2
PARTS = 4
LANES = 128
BF = jnp.bfloat16
F32 = jnp.float32


def dot_nn(left, right):
    return lax.dot_general(left, right, (((1,), (0,)), ((), ())), preferred_element_type=F32)


def dot_nt(left, right):
    return lax.dot_general(left, right, (((1,), (1,)), ((), ())), preferred_element_type=F32)


def dot_tn(left, right):
    return lax.dot_general(left, right, (((0,), (0,)), ((), ())), preferred_element_type=F32)


def iota(shape, dim):
    return lax.broadcasted_iota(jnp.int32, shape, dim)


def routing(ids, experts):
    tokens, top = ids.shape
    lane = iota((tokens, experts), 1)
    member = jnp.zeros((tokens, experts), F32)
    for k in range(top):
        member = member + jnp.where(ids[:, k : k + 1] == lane, 1.0, 0.0)
    earlier = jnp.where(iota((tokens, tokens), 1) < iota((tokens, tokens), 0), 1.0, 0.0).astype(BF)
    slot = dot_nn(earlier, member.astype(BF))
    return jnp.where(member > 0.5, slot, -1.0)


def per_row(by_expert):
    experts, width = by_expert.shape
    return jnp.broadcast_to(by_expert[:, None, :], (experts, SLOTS, width)).reshape(
        experts * SLOTS, width
    )


def dispatch_kernel(ids_ref, grad_ref, hid_ref, gain_ref, out_ref, rows_ref, parts_ref, slot_ref):
    tokens, width = grad_ref.shape
    experts = slot_ref.shape[0]
    step = pl.program_id(0)
    block_experts = out_ref.shape[0] // SLOTS
    piece = 2 * width // PARTS

    @pl.when(step == 0)
    def _():
        hid = hid_ref[...].astype(F32)
        inv_rms = lax.rsqrt(jnp.mean(hid * hid, axis=1, keepdims=True) + 1e-06)
        normed = (hid * inv_rms * gain_ref[...]).astype(BF)
        grad = grad_ref[...]
        rows_ref[:, :width] = grad
        rows_ref[:, width:] = normed
        half = PARTS // 2
        for part in range(half):
            parts_ref[part * tokens : (part + 1) * tokens, :] = grad[
                :, part * piece : (part + 1) * piece
            ]
            parts_ref[(half + part) * tokens : (half + part + 1) * tokens, :] = normed[
                :, part * piece : (part + 1) * piece
            ]
        slot_ref[...] = routing(ids_ref[...], experts).T

    start = pl.multiple_of(step * block_experts, block_experts)
    slot = per_row(slot_ref[pl.ds(start, block_experts), :])
    place = iota(slot.shape, 0) & (SLOTS - 1)
    pick = jnp.where(slot == place.astype(F32), 1.0, 0.0).astype(BF)
    chunk = 1024
    for col in range(0, 2 * width, chunk):
        out_ref[:, col : col + chunk] = dot_nn(pick, rows_ref[:, col : col + chunk]).astype(BF)
    late = slot == (SLOTS + (place >> 2)).astype(F32)
    pick_late = jnp.concatenate(
        [
            jnp.where(late & ((place & (PARTS - 1)) == part), 1.0, 0.0).astype(BF)
            for part in range(PARTS)
        ],
        axis=1,
    )
    out_ref[:, 2 * width :] = dot_nn(pick_late, parts_ref[...]).astype(BF)


def dispatch(ids, grad_out, hidden_in, gain, experts):
    tokens, width = grad_out.shape
    total = 2 * width + 2 * width // PARTS
    steps = 4
    rows = experts * SLOTS
    whole = lambda shape: pl.BlockSpec(shape, lambda i: (0,) * len(shape))
    return pl.pallas_call(
        dispatch_kernel,
        out_shape=jax.ShapeDtypeStruct((rows, total), BF),
        grid=(steps,),
        in_specs=[
            whole(ids.shape),
            whole(grad_out.shape),
            whole(hidden_in.shape),
            whole(gain.shape),
        ],
        out_specs=pl.BlockSpec((rows // steps, total), lambda i: (i, 0)),
        scratch_shapes=[
            pltpu.VMEM((tokens, 2 * width), BF),
            pltpu.VMEM((PARTS * tokens, 2 * width // PARTS), BF),
            pltpu.VMEM((experts, tokens), F32),
        ],
        compiler_params=pltpu.CompilerParams(vmem_limit_bytes=32 << 20),
        name="dispatch",
    )(ids, grad_out, hidden_in, gain)


def expert_kernel(
    rows_ref, gate_hbm, up_hbm, down_hbm, out_ref, grad_ref, norm_ref, gate_ref, up_ref, down_ref, sems
):
    width = gate_ref.shape[0]
    main = rows_ref.shape[0]
    late = main // SLOTS * EXTRA
    half = width // 2
    step = pl.program_id(0)
    loads = [
        pltpu.make_async_copy(gate_hbm, gate_ref, sems.at[0]),
        pltpu.make_async_copy(up_hbm, up_ref, sems.at[1]),
        pltpu.make_async_copy(down_hbm, down_ref, sems.at[2]),
    ]

    def first(action):
        @pl.when(step == 0)
        def _():
            action()

    first(lambda: [load.start() for load in loads])
    grad_ref[:main, :] = rows_ref[:, :width]
    norm_ref[:main, :] = rows_ref[:, width : 2 * width]
    order = iota((main, main), 0)
    source = (order % late) * PARTS + order // late
    gather = jnp.where(iota((main, main), 1) == source, 1.0, 0.0).astype(BF)
    moved = dot_nn(gather, rows_ref[:, 2 * width :]).astype(BF)
    for part in range(2):
        cols = slice(part * half, (part + 1) * half)
        grad_ref[main:, cols] = moved[part * late : (part + 1) * late]
        norm_ref[main:, cols] = moved[(2 + part) * late : (3 + part) * late]
    first(loads[0].wait)
    gate_pre = dot_nn(norm_ref[...], gate_ref[...])
    first(loads[1].wait)
    up_pre = dot_nn(norm_ref[...], up_ref[...])
    sigma = jax.nn.sigmoid(gate_pre)
    act = gate_pre * sigma
    slope = sigma * (1.0 + gate_pre * (1.0 - sigma))
    first(loads[2].wait)
    grad_hid = dot_nt(grad_ref[...], down_ref[...])
    grad_uppre = grad_hid * act
    score = jnp.sum(grad_uppre * up_pre, axis=1, keepdims=True)
    grad_gatepre = (grad_hid * up_pre * slope).astype(BF)
    grad_uppre = grad_uppre.astype(BF)
    pair = (dot_nt(grad_gatepre, gate_ref[...]) + dot_nt(grad_uppre, up_ref[...])).astype(BF)
    out_ref[:, :width] = pair[:main]
    quarter = width // PARTS
    stacked = jnp.concatenate(
        [pair[main:, part * quarter : (part + 1) * quarter] for part in range(PARTS)], axis=0
    )
    order = iota((main, main), 1)
    scatter = jnp.where(
        iota((main, main), 0) == (order % late) * PARTS + order // late, 1.0, 0.0
    ).astype(BF)
    out_ref[:, width : width + quarter] = dot_nn(scatter, stacked).astype(BF)
    spread = jnp.where((iota((main, late), 0) >> 2) == iota((main, late), 1), 1.0, 0.0).astype(BF)
    late_score = dot_nn(spread, jnp.broadcast_to(score[main:], (late, LANES)).astype(BF))
    lane = iota((main, LANES), 1)
    out_ref[:, width + quarter :] = jnp.where(
        lane == 0, score[:main], jnp.where(lane == 1, late_score, 0.0)
    ).astype(BF)


def expert_backward(arrived, gate_mat, up_mat, down_mat, steps=4):
    rows, total = arrived.shape
    width = gate_mat.shape[0]
    main = rows // steps
    both = main + main // SLOTS * EXTRA
    out_width = width + width // PARTS + LANES
    raw = pl.BlockSpec(memory_space=pl.ANY)
    return pl.pallas_call(
        expert_kernel,
        out_shape=jax.ShapeDtypeStruct((rows, out_width), BF),
        grid=(steps,),
        in_specs=[pl.BlockSpec((main, total), lambda i: (i, 0)), raw, raw, raw],
        out_specs=pl.BlockSpec((main, out_width), lambda i: (i, 0)),
        scratch_shapes=[
            pltpu.VMEM((both, width), BF),
            pltpu.VMEM((both, width), BF),
            pltpu.VMEM(gate_mat.shape, BF),
            pltpu.VMEM(up_mat.shape, BF),
            pltpu.VMEM(down_mat.shape, BF),
            pltpu.SemaphoreType.DMA((3,)),
        ],
        compiler_params=pltpu.CompilerParams(vmem_limit_bytes=56 << 20),
        name="expert",
    )(arrived, gate_mat, up_mat, down_mat)


def combine_rows(ids_ref, weight_ref, grad_ref, hid_ref, gain_ref, back_ref, out_ref, gate_ref):
    tokens, width = grad_ref.shape
    rows = back_ref.shape[0]
    experts = rows // SLOTS
    quarter = width // PARTS
    ids = ids_ref[...]
    weights = weight_ref[...]
    top = ids.shape[1]
    lane = iota((tokens, experts), 1)
    weight = jnp.zeros((tokens, experts), F32)
    for k in range(top):
        weight = weight + jnp.where(ids[:, k : k + 1] == lane, weights[:, k : k + 1], 0.0)
    slot = per_row(routing(ids, experts).T)
    weight = per_row(weight.T)
    place = iota(slot.shape, 0) & (SLOTS - 1)
    first = slot == place.astype(F32)
    late = slot == (SLOTS + (place >> 2)).astype(F32)
    high = weight.astype(BF).astype(F32)
    low = weight - high
    pick = jnp.concatenate(
        [jnp.where(first, high, 0.0).astype(BF), jnp.where(first, low, 0.0).astype(BF)], axis=1
    )
    moe = dot_tn(pick, back_ref[:, :width])
    moe = moe[:tokens] + moe[tokens:]
    pick_late = jnp.concatenate(
        [
            jnp.where(late & ((place & (PARTS - 1)) == part), value, 0.0).astype(BF)
            for part in range(PARTS)
            for value in (high, low)
        ],
        axis=1,
    )
    moe_late = dot_tn(pick_late, back_ref[:, width : width + quarter])
    moe_late = jnp.concatenate(
        [
            moe_late[2 * part * tokens : (2 * part + 1) * tokens]
            + moe_late[(2 * part + 1) * tokens : (2 * part + 2) * tokens]
            for part in range(PARTS)
        ],
        axis=1,
    )
    moe = moe + moe_late
    hid = hid_ref[...].astype(F32)
    inv_rms = lax.rsqrt(jnp.mean(hid * hid, axis=1, keepdims=True) + 1e-06)
    normal = hid * inv_rms
    scaled = moe * gain_ref[...]
    inner_mean = jnp.mean(scaled * normal, axis=1, keepdims=True)
    out_ref[...] = (grad_ref[...].astype(F32) + inv_rms * (scaled - normal * inner_mean)).astype(BF)
    score = back_ref[:, width + quarter :].astype(F32)
    got = jnp.where(first, score[:, 0:1], 0.0) + jnp.where(
        late & ((place & (PARTS - 1)) == 0), score[:, 1:2], 0.0
    )
    by_expert = jnp.sum(got.reshape(experts, SLOTS, tokens), axis=1).T
    column = iota((tokens, top), 1)
    gate = jnp.zeros((tokens, top), F32)
    for k in range(top):
        value = jnp.sum(jnp.where(ids[:, k : k + 1] == lane, by_expert, 0.0), axis=1, keepdims=True)
        gate = gate + jnp.where(column == k, value, 0.0)
    gate_ref[...] = gate.astype(BF)


def combine_kernel(
    ids_ref,
    weight_ref,
    grad_ref,
    hid_ref,
    gain_ref,
    back_ref,
    proj_ref,
    out_ref,
    gate_ref,
    attn_ref,
):
    @pl.when(pl.program_id(0) == 0)
    def _():
        combine_rows(
            ids_ref, weight_ref, grad_ref, hid_ref, gain_ref, back_ref, out_ref, gate_ref
        )

    pieces, _, piece, width = proj_ref.shape
    owners, heads, tokens, _ = attn_ref.shape
    each = pieces // owners
    for owner in range(owners):
        proj = proj_ref[:, owner].reshape(pieces * piece, width)
        grad = dot_nt(out_ref[...], proj).astype(BF)
        for head in range(heads):
            attn_ref[owner, head] = grad[:, head * HD : (head + 1) * HD]


def combine(ids, weights, grad_out, hidden_in, gain, back, proj):
    tokens, width = grad_out.shape
    pieces, owners, piece, _ = proj.shape
    heads = pieces * piece // HD
    group = 2
    whole = lambda shape: pl.BlockSpec(shape, lambda i: (0,) * len(shape))
    return pl.pallas_call(
        combine_kernel,
        out_shape=(
            jax.ShapeDtypeStruct(grad_out.shape, BF),
            jax.ShapeDtypeStruct(ids.shape, BF),
            jax.ShapeDtypeStruct((owners, heads, tokens, HD), BF),
        ),
        grid=(owners // group,),
        in_specs=[
            whole(ids.shape),
            whole(weights.shape),
            whole(grad_out.shape),
            whole(hidden_in.shape),
            whole(gain.shape),
            whole(back.shape),
            pl.BlockSpec((pieces, group, piece, width), lambda i: (0, i, 0, 0)),
        ],
        out_specs=(
            whole(grad_out.shape),
            whole(ids.shape),
            pl.BlockSpec((group, heads, tokens, HD), lambda i: (i, 0, 0, 0)),
        ),
        compiler_params=pltpu.CompilerParams(vmem_limit_bytes=48 << 20),
        name="combine",
    )(ids, weights, grad_out, hidden_in, gain, back, proj)


BLOCK = 256


def probs_kernel(q_ref, k_ref, out_ref):
    length = q_ref.shape[0]
    scale = HD ** (-0.5)
    start = 0
    for lo in range(0, length, BLOCK):
        hi = lo + BLOCK
        scores = dot_nt(k_ref[:hi, :], q_ref[lo:hi, :])
        corner = jnp.where(
            iota((BLOCK, BLOCK), 0) <= iota((BLOCK, BLOCK), 1), scores[lo:], -jnp.inf
        )
        scores = jnp.concatenate([scores[:lo], corner], axis=0) if lo else corner
        peak = jnp.max(scores, axis=0, keepdims=True)
        exp_scores = jnp.exp((scores - peak) * scale)
        total = jnp.sum(exp_scores, axis=0, keepdims=True)
        out_ref[start : start + hi, :] = (exp_scores * (1.0 / total)).astype(BF)
        start += hi


def packed_rows(length):
    return sum(range(BLOCK, length + 1, BLOCK))


def attention_probs(query, key):
    tokens, cols = query.shape
    length = tokens // SEQS
    heads = cols // HD
    item = pl.BlockSpec((length, HD), lambda s, h: (s, h))
    return pl.pallas_call(
        probs_kernel,
        out_shape=jax.ShapeDtypeStruct((SEQS, heads, packed_rows(length), BLOCK), BF),
        grid=(SEQS, heads),
        in_specs=[item, item],
        out_specs=pl.BlockSpec((None, None, packed_rows(length), BLOCK), lambda s, h: (s, h, 0, 0)),
        compiler_params=pltpu.CompilerParams(vmem_limit_bytes=32 << 20),
        name="probs",
    )(query, key)


def attention_kernel(probs_ref, grad_ref, q_ref, k_ref, v_ref, dq_ref, dk_ref, dv_ref, acc_k, acc_v):
    length = q_ref.shape[0]
    scale = HD ** (-0.5)
    grad_all = grad_ref[...].reshape(length, HD)
    start = 0
    for lo in range(0, length, BLOCK):
        hi = lo + BLOCK
        query = q_ref[lo:hi, :]
        grad = grad_all[lo:hi]
        probs = probs_ref[start : start + hi, :]
        start += hi
        full = probs.astype(F32)
        grad_probs = dot_nt(v_ref[:hi, :], grad)
        delta = jnp.sum(full * grad_probs, axis=0, keepdims=True)
        grad_scores = (full * (grad_probs - delta)).astype(BF)
        dq_ref[lo:hi, :] = (scale * dot_tn(grad_scores, k_ref[:hi, :])).astype(BF)
        dv = dot_nn(probs, grad)
        dk = dot_nn(grad_scores, query)
        if lo:
            acc_k[:lo, :] += dk[:lo]
            acc_v[:lo, :] += dv[:lo]
        acc_k[lo:hi, :] = dk[lo:]
        acc_v[lo:hi, :] = dv[lo:]
    dk_ref[...] = (scale * acc_k[...]).astype(BF)
    dv_ref[...] = acc_v[...].astype(BF)


def attention(probs, grad_attn, query, key, value):
    tokens, cols = query.shape
    length = tokens // SEQS
    owners, _, part, _ = grad_attn.shape
    item = pl.BlockSpec((length, HD), lambda s, h: (s, h))
    return pl.pallas_call(
        attention_kernel,
        out_shape=[jax.ShapeDtypeStruct(query.shape, BF)] * 3,
        grid=(SEQS, cols // HD),
        in_specs=[
            pl.BlockSpec((None, None) + probs.shape[2:], lambda s, h: (s, h, 0, 0)),
            pl.BlockSpec((owners // SEQS, None, part, HD), lambda s, h: (s, h, 0, 0)),
            item,
            item,
            item,
        ],
        out_specs=[item] * 3,
        scratch_shapes=[pltpu.VMEM((length, HD), F32), pltpu.VMEM((length, HD), F32)],
        compiler_params=pltpu.CompilerParams(vmem_limit_bytes=32 << 20),
        name="attention",
    )(probs, grad_attn, query, key, value)


def exchange(rows, experts):
    total = rows.shape[1]
    moved = lax.all_to_all(
        rows.reshape(experts, SLOTS, total),
        ("group", "inner"),
        split_axis=0,
        concat_axis=0,
        tiled=True,
    )
    return moved.reshape(experts * SLOTS, total)


def local(
    grad_out,
    hidden_in,
    norm_gain,
    expert_ids,
    gate_weights,
    gate_proj,
    up_proj,
    down_proj,
    out_proj,
    query_rows,
    key_rows,
    value_rows,
):
    groups = lax.axis_size("group")
    owners = lax.axis_size("inner")
    experts = groups * owners
    gain = norm_gain.reshape(1, -1)
    tokens, width = grad_out.shape
    piece = out_proj.shape[0] // groups
    own_proj = lax.dynamic_slice_in_dim(out_proj, lax.axis_index("group") * piece, piece, 0)
    proj = lax.all_gather(own_proj, ("group", "inner"), axis=0, tiled=False)
    outgoing = dispatch(expert_ids, grad_out, hidden_in, gain, experts)
    outgoing, query_late = lax.optimization_barrier((outgoing, query_rows))
    arrived = exchange(outgoing, experts)
    probs = attention_probs(query_late, key_rows)
    arrived, probs = lax.optimization_barrier((arrived, probs))
    answers = expert_backward(arrived, gate_proj[0], up_proj[0], down_proj[0])
    back = exchange(answers, experts)
    grad_hidden, grad_gate, grad_attn = combine(
        expert_ids,
        gate_weights,
        grad_out,
        hidden_in,
        gain,
        back,
        proj.reshape(groups, owners, piece, width),
    )
    heads = grad_attn.shape[1]
    grad_attn = lax.all_to_all(
        grad_attn.reshape(owners, heads * tokens, HD),
        "inner",
        split_axis=0,
        concat_axis=0,
        tiled=True,
    )
    grad_q, grad_k, grad_v = attention(
        probs, grad_attn.reshape(owners, heads, tokens, HD), query_rows, key_rows, value_rows
    )
    return (grad_hidden, grad_gate, grad_q, grad_k, grad_v)


def solution(mesh):
    rows = P(("group", "inner"), None)
    stack = P(("group", "inner"), None, None)
    heads = P("group", "inner")
    return jax.shard_map(
        local,
        mesh=mesh,
        in_specs=(
            rows,
            rows,
            P(),
            rows,
            rows,
            stack,
            stack,
            stack,
            P("inner", None),
            heads,
            heads,
            heads,
        ),
        out_specs=(rows, rows, heads, heads, heads),
        check_vma=False,
    )
```

```python
import functools

import jax
import jax.numpy as jnp
from jax import lax
from jax.experimental import pallas as pl
from jax.experimental.pallas import tpu as pltpu
from jax.sharding import PartitionSpec as P

HD = 128
SEQS = 2
SLOTS = 8
EXTRA = 2
PARTS = 4
LANES = 128
BF = jnp.bfloat16
F32 = jnp.float32


def dot_nn(left, right):
    return lax.dot_general(left, right, (((1,), (0,)), ((), ())), preferred_element_type=F32)


def dot_nt(left, right):
    return lax.dot_general(left, right, (((1,), (1,)), ((), ())), preferred_element_type=F32)


def dot_tn(left, right):
    return lax.dot_general(left, right, (((0,), (0,)), ((), ())), preferred_element_type=F32)


HELD = pl.BlockSpec(memory_space=pltpu.VMEM)
RAW = pl.BlockSpec(memory_space=pl.ANY)


def kernel_call(kernel, out_shape, vmem, space=pltpu.HBM, free=(), **fields):
    outs = out_shape
    if space is not None:
        outs = jax.tree.map(lambda out: space(out.shape, out.dtype), out_shape)
    call = pl.pallas_call(
        kernel,
        out_shape=outs,
        compiler_params=pltpu.CompilerParams(vmem_limit_bytes=vmem << 20),
        **fields,
    )
    pin = lambda arg: pltpu.with_memory_space_constraint(arg, pltpu.HBM)
    return lambda *args: call(*[arg if n in free else pin(arg) for n, arg in enumerate(args)])


def iota(shape, dim):
    return lax.broadcasted_iota(jnp.int32, shape, dim)


def routing(ids, experts):
    tokens, top = ids.shape
    lane = iota((tokens, experts), 1)
    member = jnp.zeros((tokens, experts), F32)
    for k in range(top):
        member = member + jnp.where(ids[:, k : k + 1] == lane, 1.0, 0.0)
    earlier = jnp.where(iota((tokens, tokens), 1) < iota((tokens, tokens), 0), 1.0, 0.0).astype(BF)
    slot = dot_nn(earlier, member.astype(BF))
    return jnp.where(member > 0.5, slot, -1.0)


def per_row(by_expert):
    experts, width = by_expert.shape
    return jnp.broadcast_to(by_expert[:, None, :], (experts, SLOTS, width)).reshape(
        experts * SLOTS, width
    )


def dispatch_kernel(ids_ref, grad_ref, hid_ref, gain_ref, out_ref, rows_ref, parts_ref, slot_ref):
    tokens, width = grad_ref.shape
    experts = slot_ref.shape[0]
    step = pl.program_id(0)
    block_experts = out_ref.shape[0] // SLOTS
    piece = 2 * width // PARTS

    @pl.when(step == 0)
    def _():
        hid = hid_ref[...].astype(F32)
        inv_rms = lax.rsqrt(jnp.mean(hid * hid, axis=1, keepdims=True) + 1e-06)
        normed = (hid * inv_rms * gain_ref[...]).astype(BF)
        grad = grad_ref[...]
        rows_ref[:, :width] = grad
        rows_ref[:, width:] = normed
        half = PARTS // 2
        for part in range(half):
            parts_ref[part * tokens : (part + 1) * tokens, :] = grad[
                :, part * piece : (part + 1) * piece
            ]
            parts_ref[(half + part) * tokens : (half + part + 1) * tokens, :] = normed[
                :, part * piece : (part + 1) * piece
            ]
        slot_ref[...] = routing(ids_ref[...], experts).T

    start = pl.multiple_of(step * block_experts, block_experts)
    slot = per_row(slot_ref[pl.ds(start, block_experts), :])
    place = iota(slot.shape, 0) & (SLOTS - 1)
    pick = jnp.where(slot == place.astype(F32), 1.0, 0.0).astype(BF)
    chunk = 1024
    for col in range(0, 2 * width, chunk):
        out_ref[:, col : col + chunk] = dot_nn(pick, rows_ref[:, col : col + chunk]).astype(BF)
    late = slot == (SLOTS + (place >> 2)).astype(F32)
    pick_late = jnp.concatenate(
        [
            jnp.where(late & ((place & (PARTS - 1)) == part), 1.0, 0.0).astype(BF)
            for part in range(PARTS)
        ],
        axis=1,
    )
    out_ref[:, 2 * width :] = dot_nn(pick_late, parts_ref[...]).astype(BF)


def dispatch(ids, grad_out, hidden_in, gain, experts):
    tokens, width = grad_out.shape
    total = 2 * width + 2 * width // PARTS
    steps = 4
    rows = experts * SLOTS
    return kernel_call(
        dispatch_kernel,
        out_shape=jax.ShapeDtypeStruct((rows, total), BF),
        grid=(steps,),
        in_specs=[
            whole(ids.shape),
            whole(grad_out.shape),
            whole(hidden_in.shape),
            whole(gain.shape),
        ],
        out_specs=pl.BlockSpec((rows // steps, total), lambda i: (i, 0)),
        scratch_shapes=[
            pltpu.VMEM((tokens, 2 * width), BF),
            pltpu.VMEM((PARTS * tokens, 2 * width // PARTS), BF),
            pltpu.VMEM((experts, tokens), F32),
        ],
        vmem=16,
        name="dispatch",
    )(ids, grad_out, hidden_in, gain)


def expert_kernel(
    rows_hbm,
    gate_hbm,
    up_hbm,
    down_hbm,
    out_hbm,
    rows_ref,
    gate_ref,
    up_ref,
    down_ref,
    late_ref,
    act_ref,
    out_ref,
    in_sems,
    out_sems,
):
    width, hidden = gate_ref.shape
    rows = rows_ref.shape[0]
    group = rows // 2
    late = group // SLOTS * EXTRA
    quarter = width // PARTS
    chunk = 256

    def fetch(source, target, n):
        copy = pltpu.make_async_copy(source, target, in_sems.at[n])
        copy.start()
        return copy

    def columns(lo, first, last, n):
        at = (slice(lo, lo + group), slice(first, last))
        return fetch(rows_hbm.at[at], rows_ref.at[at], n)

    norm_0 = columns(0, width, 2 * width, 0)
    gate_in = fetch(gate_hbm, gate_ref, 1)
    up_in = fetch(up_hbm, up_ref, 2)
    grad_0 = columns(0, 0, width, 3)
    down_in = fetch(down_hbm, down_ref, 4)
    all_1 = columns(group, 0, 2 * width, 5)
    late_0 = columns(0, 2 * width, 2 * width + 2 * quarter, 6)
    late_1 = columns(group, 2 * width, 2 * width + 2 * quarter, 7)

    def backward(norm, grad, before_up=(), before_grad=(), acts=None):
        gate_pre = dot_nn(norm(), gate_ref[...])
        for copy in before_up:
            copy.wait()
        up_pre = dot_nn(norm(), up_ref[...])
        for copy in before_grad:
            copy.wait()
        score = None
        for col in range(0, hidden, chunk):
            cols = slice(col, col + chunk)
            grad_hid = dot_nt(grad(), down_ref[cols, :])
            gate_part = gate_pre[:, cols]
            sigma = jax.nn.sigmoid(gate_part)
            act = gate_part * sigma
            slope = sigma * (1.0 + gate_part * (1.0 - sigma))
            grad_up = grad_hid * up_pre[:, cols]
            partial = jnp.sum(grad_up * act, axis=1, keepdims=True)
            score = partial if score is None else score + partial
            acts[:, cols] = (grad_up * slope).astype(BF)
            acts[:, hidden + col : hidden + col + chunk] = (grad_hid * act).astype(BF)
        return score

    def pair(acts, cols):
        total = dot_nt(acts[:, :hidden], gate_ref[cols, :])
        return (total + dot_nt(acts[:, hidden:], up_ref[cols, :])).astype(BF)

    sent = []

    def send(lo, height, first, last):
        at = (slice(lo, lo + height), slice(first, last))
        copy = pltpu.make_async_copy(out_ref.at[at], out_hbm.at[at], out_sems.at[len(sent)])
        copy.start()
        sent.append(copy)

    main_scores = []
    for index in range(2):
        at = slice(index * group, (index + 1) * group)
        if index == 0:
            norm_0.wait()
            gate_in.wait()
            waits = ((up_in,), (grad_0, down_in))
        else:
            all_1.wait()
            waits = ((), ())
        acts = act_ref.at[at]
        main_scores.append(
            backward(
                lambda: rows_ref[at, width : 2 * width], lambda: rows_ref[at, :width], *waits, acts
            )
        )
        for col in range(0, width, quarter):
            cols = slice(col, col + quarter)
            out_ref[at, cols] = pair(acts, cols)
        send(index * group, group, 0, width)

    late_0.wait()
    late_1.wait()
    half = group // 2
    few = half // SLOTS * EXTRA
    order = iota((half, half), 0)
    source = (order % few) * PARTS + order // few
    gather = jnp.where(iota((half, half), 1) == source, 1.0, 0.0).astype(BF)
    for block in range(rows // half):
        moved = dot_nn(gather, rows_ref[block * half : (block + 1) * half, 2 * width :]).astype(BF)
        for part in range(PARTS):
            late_ref[block * few : (block + 1) * few, part * 2 * quarter : (part + 1) * 2 * quarter] = (
                moved[part * few : (part + 1) * few]
            )
    acts = act_ref.at[rows:]
    late_score = backward(
        lambda: late_ref[:, width : 2 * width], lambda: late_ref[:, :width], acts=acts
    )
    ends = [pair(acts, slice(col, col + quarter)) for col in range(0, width, quarter)]
    order = iota((half, half), 1)
    scatter = jnp.where(
        iota((half, half), 0) == (order % few) * PARTS + order // few, 1.0, 0.0
    ).astype(BF)
    spread = jnp.where((iota((half, few), 0) >> 2) == iota((half, few), 1), 1.0, 0.0).astype(BF)
    lane = iota((half, LANES), 1)
    for block in range(rows // half):
        at = slice(block * half, (block + 1) * half)
        own = slice(block * few, (block + 1) * few)
        stacked = jnp.concatenate([end[own] for end in ends], axis=0)
        out_ref[at, width : width + quarter] = dot_nn(scatter, stacked).astype(BF)
        spread_score = dot_nn(spread, jnp.broadcast_to(late_score[own], (few, LANES)).astype(BF))
        start = (block % 2) * half
        main_score = main_scores[block // 2][start : start + half]
        out_ref[at, width + quarter :] = jnp.where(
            lane == 0, main_score, jnp.where(lane == 1, spread_score, 0.0)
        ).astype(BF)
    send(0, rows, width, width + quarter + LANES)
    for copy in sent:
        copy.wait()


def expert_backward(arrived, gate_mat, up_mat, down_mat):
    rows = arrived.shape[0]
    width, hidden = gate_mat.shape
    late = rows // SLOTS * EXTRA
    out_shape = (rows, width + width // PARTS + LANES)
    return kernel_call(
        expert_kernel,
        out_shape=jax.ShapeDtypeStruct(out_shape, BF),
        in_specs=[RAW] * 4,
        out_specs=RAW,
        scratch_shapes=[
            pltpu.VMEM(arrived.shape, BF),
            pltpu.VMEM(gate_mat.shape, BF),
            pltpu.VMEM(up_mat.shape, BF),
            pltpu.VMEM(down_mat.shape, BF),
            pltpu.VMEM((late, 2 * width), BF),
            pltpu.VMEM((rows + late, 2 * hidden), BF),
            pltpu.VMEM(out_shape, BF),
            pltpu.SemaphoreType.DMA((8,)),
            pltpu.SemaphoreType.DMA((3,)),
        ],
        vmem=58,
        name="expert",
    )(arrived, gate_mat, up_mat, down_mat)


def whole(shape):
    return pl.BlockSpec(shape, lambda i: (0,) * len(shape))


def placed(ids, rows):
    experts = rows // SLOTS
    slot = per_row(routing(ids, experts).T)
    place = iota(slot.shape, 0) & (SLOTS - 1)
    return slot == place.astype(F32), slot == (SLOTS + (place >> 2)).astype(F32), place


def plan_kernel(ids_ref, weight_ref, first_ref, late_ref):
    ids = ids_ref[...]
    weights = weight_ref[...]
    tokens, top = ids.shape
    rows = first_ref.shape[1]
    experts = rows // SLOTS
    lane = iota((tokens, experts), 1)
    weight = jnp.zeros((tokens, experts), F32)
    for k in range(top):
        weight = weight + jnp.where(ids[:, k : k + 1] == lane, weights[:, k : k + 1], 0.0)
    weight = per_row(weight.T)
    first, late, place = placed(ids, rows)
    high = weight.astype(BF).astype(F32)
    for n, value in enumerate((high, weight - high)):
        first_ref[n * tokens : (n + 1) * tokens, :] = jnp.where(first, value, 0.0).T.astype(BF)
        for part in range(PARTS):
            start = (2 * part + n) * tokens
            hit = late & ((place & (PARTS - 1)) == part)
            late_ref[start : start + tokens, :] = jnp.where(hit, value, 0.0).T.astype(BF)


def plan(ids, weights, experts):
    tokens = ids.shape[0]
    rows = experts * SLOTS
    return kernel_call(
        plan_kernel,
        out_shape=(
            jax.ShapeDtypeStruct((2 * tokens, rows), BF),
            jax.ShapeDtypeStruct((2 * PARTS * tokens, rows), BF),
        ),
        space=pltpu.VMEM,
        vmem=16,
        name="plan",
    )(ids, weights)


def combine_kernel(
    first_ref,
    late_ref,
    grad_ref,
    hid_ref,
    gain_ref,
    back_hbm,
    proj_hbm,
    out_ref,
    attn_ref,
    back_ref,
    proj_ref,
    sems,
):
    tokens, width = grad_ref.shape
    quarter = width // PARTS
    pieces, owners, piece, _ = proj_ref.shape
    group = owners // 8
    heads = attn_ref.shape[1]

    def fetch(source, target, n):
        copy = pltpu.make_async_copy(source, target, sems.at[n])
        copy.start()
        return copy

    backs = []
    for n, part in enumerate((PARTS,) + tuple(range(PARTS))):
        at = (slice(None), slice(part * quarter, (part + 1) * quarter))
        backs.append(fetch(back_hbm.at[at], back_ref.at[at], n))
    def proj_copy(n):
        at = (slice(None), pl.ds(n * group, group))
        return pltpu.make_async_copy(proj_hbm.at[at], proj_ref.at[at], sems.at[len(backs) + n])

    for n in range(8):
        proj_copy(n).start()

    hid = hid_ref[...].astype(F32)
    inv_rms = lax.rsqrt(jnp.mean(hid * hid, axis=1, keepdims=True) + 1e-06)
    backs[0].wait()
    late = dot_nn(late_ref[...], back_ref[:, width:])
    total = jnp.zeros((tokens, 1), F32)
    parts = []
    for part in range(PARTS):
        cols = slice(part * quarter, (part + 1) * quarter)
        backs[1 + part].wait()
        moe = dot_nn(first_ref[...], back_ref[:, cols])
        begin = 2 * part * tokens
        moe = (moe[:tokens] + moe[tokens:]) + (
            late[begin : begin + tokens] + late[begin + tokens : begin + 2 * tokens]
        )
        scaled = moe * gain_ref[:, cols]
        parts.append(scaled)
        total = total + jnp.sum(scaled * (hid[:, cols] * inv_rms), axis=1, keepdims=True)
    inner_mean = total * (1.0 / width)
    for part in range(PARTS):
        cols = slice(part * quarter, (part + 1) * quarter)
        change = parts[part] - hid[:, cols] * inv_rms * inner_mean
        out_ref[:, cols] = (grad_ref[:, cols].astype(F32) + inv_rms * change).astype(BF)

    def project(n, carry):
        proj_copy(n).wait()
        for index in range(group):
            owner = n * group + index
            proj = proj_ref[:, owner].reshape(pieces * piece, width)
            grad = dot_nt(out_ref[...], proj).astype(BF)
            for head in range(heads):
                attn_ref[owner, head] = grad[:, head * HD : (head + 1) * HD]
        return carry

    lax.fori_loop(0, 8, project, 0)


def combine(first, late, grad_out, hidden_in, gain, back, proj):
    tokens, width = grad_out.shape
    pieces, owners, piece, _ = proj.shape
    heads = pieces * piece // HD
    return kernel_call(
        combine_kernel,
        out_shape=(
            jax.ShapeDtypeStruct(grad_out.shape, BF),
            jax.ShapeDtypeStruct((owners, heads, tokens, HD), BF),
        ),
        in_specs=[HELD] * 5 + [RAW] * 2,
        out_specs=(HELD, HELD),
        scratch_shapes=[
            pltpu.VMEM((back.shape[0], width + width // PARTS), BF),
            pltpu.VMEM(proj.shape, BF),
            pltpu.SemaphoreType.DMA((PARTS + 9,)),
        ],
        vmem=50,
        space=None,
        free=(0, 1, 2, 3, 4),
        name="combine",
    )(first, late, grad_out, hidden_in, gain, back, proj)


def score_kernel(ids_ref, score_ref, gate_ref):
    ids = ids_ref[...]
    tokens, top = ids.shape
    rows = score_ref.shape[0]
    experts = rows // SLOTS
    score = score_ref[...].astype(F32)
    first, late, place = placed(ids, rows)
    got = jnp.where(first, score[:, 0:1], 0.0) + jnp.where(
        late & ((place & (PARTS - 1)) == 0), score[:, 1:2], 0.0
    )
    by_expert = jnp.sum(got.reshape(experts, SLOTS, tokens), axis=1).T
    lane = iota((tokens, experts), 1)
    column = iota((tokens, top), 1)
    gate = jnp.zeros((tokens, top), F32)
    for k in range(top):
        value = jnp.sum(jnp.where(ids[:, k : k + 1] == lane, by_expert, 0.0), axis=1, keepdims=True)
        gate = gate + jnp.where(column == k, value, 0.0)
    gate_ref[...] = gate.astype(BF)


def scores(ids, back):
    rows, total = back.shape
    return kernel_call(
        score_kernel,
        out_shape=jax.ShapeDtypeStruct(ids.shape, BF),
        grid=(1,),
        in_specs=[
            whole(ids.shape),
            pl.BlockSpec((rows, LANES), lambda i: (0, total // LANES - 1)),
        ],
        out_specs=whole(ids.shape),
        vmem=16,
        name="scores",
    )(ids, back)


BLOCK = 256


def probs_kernel(q_ref, k_ref, out_ref):
    length = q_ref.shape[0]
    scale = HD ** (-0.5)
    start = 0
    for lo in range(0, length, BLOCK):
        hi = lo + BLOCK
        scores = dot_nt(k_ref[:hi, :], q_ref[lo:hi, :])
        corner = jnp.where(
            iota((BLOCK, BLOCK), 0) <= iota((BLOCK, BLOCK), 1), scores[lo:], -jnp.inf
        )
        scores = jnp.concatenate([scores[:lo], corner], axis=0) if lo else corner
        peak = jnp.max(scores, axis=0, keepdims=True)
        exp_scores = jnp.exp((scores - peak) * scale)
        total = jnp.sum(exp_scores, axis=0, keepdims=True)
        out_ref[start : start + hi, :] = (exp_scores * (1.0 / total)).astype(BF)
        start += hi


def packed_rows(length):
    return sum(range(BLOCK, length + 1, BLOCK))


def attention_probs(query, key):
    tokens, cols = query.shape
    length = tokens // SEQS
    heads = cols // HD
    item = pl.BlockSpec((length, HD), lambda s, h: (s, h))
    return kernel_call(
        probs_kernel,
        out_shape=jax.ShapeDtypeStruct((SEQS, heads, packed_rows(length), BLOCK), BF),
        grid=(SEQS, heads),
        in_specs=[item, item],
        out_specs=pl.BlockSpec((None, None, packed_rows(length), BLOCK), lambda s, h: (s, h, 0, 0)),
        vmem=16,
        name="probs",
    )(query, key)


def attention_kernel(probs_ref, grad_ref, q_ref, k_ref, v_ref, dq_ref, dk_ref, dv_ref, acc_k, acc_v):
    length = q_ref.shape[0]
    scale = HD ** (-0.5)
    grad_all = grad_ref[...].reshape(length, HD)
    start = 0
    for lo in range(0, length, BLOCK):
        hi = lo + BLOCK
        query = q_ref[lo:hi, :]
        grad = grad_all[lo:hi]
        probs = probs_ref[start : start + hi, :]
        start += hi
        full = probs.astype(F32)
        grad_probs = dot_nt(v_ref[:hi, :], grad)
        delta = jnp.sum(full * grad_probs, axis=0, keepdims=True)
        grad_scores = (full * (grad_probs - delta)).astype(BF)
        dq_ref[lo:hi, :] = (scale * dot_tn(grad_scores, k_ref[:hi, :])).astype(BF)
        dv = dot_nn(probs, grad)
        dk = dot_nn(grad_scores, query)
        if lo:
            acc_k[:lo, :] += dk[:lo]
            acc_v[:lo, :] += dv[:lo]
        acc_k[lo:hi, :] = dk[lo:]
        acc_v[lo:hi, :] = dv[lo:]
    dk_ref[...] = (scale * acc_k[...]).astype(BF)
    dv_ref[...] = acc_v[...].astype(BF)


def attention(probs, grad_attn, query, key, value):
    tokens, cols = query.shape
    length = tokens // SEQS
    owners, _, part, _ = grad_attn.shape
    item = pl.BlockSpec((length, HD), lambda s, h: (s, h))
    return kernel_call(
        attention_kernel,
        out_shape=[jax.ShapeDtypeStruct(query.shape, BF)] * 3,
        grid=(SEQS, cols // HD),
        in_specs=[
            pl.BlockSpec((None, None) + probs.shape[2:], lambda s, h: (s, h, 0, 0)),
            pl.BlockSpec((owners // SEQS, None, part, HD), lambda s, h: (s, h, 0, 0)),
            item,
            item,
            item,
        ],
        out_specs=[item] * 3,
        scratch_shapes=[pltpu.VMEM((length, HD), F32), pltpu.VMEM((length, HD), F32)],
        vmem=24,
        free=(1,),
        name="attention",
    )(probs, grad_attn, query, key, value)


def exchange(rows, experts):
    total = rows.shape[1]
    moved = lax.all_to_all(
        rows.reshape(experts, SLOTS, total),
        ("group", "inner"),
        split_axis=0,
        concat_axis=0,
        tiled=True,
    )
    return moved.reshape(experts * SLOTS, total)


def local(
    grad_out,
    hidden_in,
    norm_gain,
    expert_ids,
    gate_weights,
    gate_proj,
    up_proj,
    down_proj,
    out_proj,
    query_rows,
    key_rows,
    value_rows,
):
    groups = lax.axis_size("group")
    owners = lax.axis_size("inner")
    experts = groups * owners
    gain = norm_gain.reshape(1, -1)
    tokens, width = grad_out.shape
    piece = out_proj.shape[0] // groups
    own_proj = lax.dynamic_slice_in_dim(out_proj, lax.axis_index("group") * piece, piece, 0)
    proj = lax.all_gather(own_proj, ("group", "inner"), axis=0, tiled=False)
    outgoing = dispatch(expert_ids, grad_out, hidden_in, gain, experts)
    outgoing, query = lax.optimization_barrier((outgoing, query_rows))
    arrived = exchange(outgoing, experts)
    probs = attention_probs(query, key_rows)
    arrived, probs = lax.optimization_barrier((arrived, probs))
    answers = expert_backward(arrived, gate_proj[0], up_proj[0], down_proj[0])
    answers, ids = lax.optimization_barrier((answers, expert_ids))
    back = exchange(answers, experts)
    first, late = plan(ids, gate_weights, experts)
    back, first, late = lax.optimization_barrier((back, first, late))
    grad_hidden, grad_attn = combine(
        first, late, grad_out, hidden_in, gain, back, proj.reshape(groups, owners, piece, width)
    )
    heads = grad_attn.shape[1]
    grad_attn, back = lax.optimization_barrier((grad_attn, back))
    grad_gate = scores(expert_ids, back)
    grad_attn = lax.all_to_all(
        grad_attn.reshape(owners, heads * tokens, HD),
        "inner",
        split_axis=0,
        concat_axis=0,
        tiled=True,
    )
    grad_attn, grad_gate = lax.optimization_barrier((grad_attn, grad_gate))
    grad_q, grad_k, grad_v = attention(
        probs, grad_attn.reshape(owners, heads, tokens, HD), query_rows, key_rows, value_rows
    )
    return (grad_hidden, grad_gate, grad_q, grad_k, grad_v)


def solution(mesh):
    rows = P(("group", "inner"), None)
    stack = P(("group", "inner"), None, None)
    heads = P("group", "inner")
    return jax.shard_map(
        local,
        mesh=mesh,
        in_specs=(
            rows,
            rows,
            P(),
            rows,
            rows,
            stack,
            stack,
            stack,
            P("inner", None),
            heads,
            heads,
            heads,
        ),
        out_specs=(rows, rows, heads, heads, heads),
        check_vma=False,
    )
```

```python
import functools

import jax
import jax.numpy as jnp
from jax import lax
from jax.experimental import pallas as pl
from jax.experimental.pallas import tpu as pltpu
from jax.sharding import PartitionSpec as P

HD = 128
SEQS = 2
SLOTS = 8
EXTRA = 2
PARTS = 4
LANES = 128
BF = jnp.bfloat16
F32 = jnp.float32


def dot_nn(left, right):
    return lax.dot_general(left, right, (((1,), (0,)), ((), ())), preferred_element_type=F32)


def dot_nt(left, right):
    return lax.dot_general(left, right, (((1,), (1,)), ((), ())), preferred_element_type=F32)


def dot_tn(left, right):
    return lax.dot_general(left, right, (((0,), (0,)), ((), ())), preferred_element_type=F32)


HELD = pl.BlockSpec(memory_space=pltpu.VMEM)
RAW = pl.BlockSpec(memory_space=pl.ANY)


def kernel_call(kernel, out_shape, vmem, space=pltpu.HBM, free=(), **fields):
    outs = out_shape
    if space is not None:
        outs = jax.tree.map(lambda out: space(out.shape, out.dtype), out_shape)
    call = pl.pallas_call(
        kernel,
        out_shape=outs,
        compiler_params=pltpu.CompilerParams(vmem_limit_bytes=vmem << 20),
        **fields,
    )
    pin = lambda arg: pltpu.with_memory_space_constraint(arg, pltpu.HBM)
    return lambda *args: call(*[arg if n in free else pin(arg) for n, arg in enumerate(args)])


def whole(shape):
    return pl.BlockSpec(shape, lambda i: (0,) * len(shape))


def iota(shape, dim):
    return lax.broadcasted_iota(jnp.int32, shape, dim)


def routing(ids, experts):
    top, tokens = ids.shape
    row = iota((experts, tokens), 0)
    member = jnp.zeros((experts, tokens), F32)
    for k in range(top):
        member = member + jnp.where(ids[k : k + 1, :] == row, 1.0, 0.0)
    earlier = jnp.where(iota((tokens, tokens), 0) < iota((tokens, tokens), 1), 1.0, 0.0).astype(BF)
    slot = dot_nn(member.astype(BF), earlier)
    return jnp.where(member > 0.5, slot, -1.0)


def per_row(by_expert):
    experts, width = by_expert.shape
    return jnp.broadcast_to(by_expert[:, None, :], (experts, SLOTS, width)).reshape(
        experts * SLOTS, width
    )


def own_rows_kernel(place_ref, proj_hbm, own_hbm, sem):
    piece = own_hbm.shape[0]
    begin = pl.multiple_of(place_ref[0] * piece, piece)
    own = pltpu.make_async_copy(proj_hbm.at[pl.ds(begin, piece)], own_hbm, sem)
    own.start()
    own.wait()


def own_rows(place, proj, pieces):
    return kernel_call(
        own_rows_kernel,
        out_shape=jax.ShapeDtypeStruct((proj.shape[0] // pieces, proj.shape[1]), BF),
        in_specs=[pl.BlockSpec(memory_space=pltpu.SMEM), RAW],
        out_specs=RAW,
        scratch_shapes=[pltpu.SemaphoreType.DMA(())],
        vmem=16,
        free=(0,),
        name="own_rows",
    )(place, proj)


def dispatch_kernel(ids_ref, grad_ref, hid_ref, gain_ref, out_ref, rows_ref, parts_ref, slot_ref):
    tokens, width = grad_ref.shape
    experts = slot_ref.shape[0]
    step = pl.program_id(0)
    block_experts = out_ref.shape[0] // SLOTS
    piece = 2 * width // PARTS

    @pl.when(step == 0)
    def _():
        hid = hid_ref[...].astype(F32)
        inv_rms = lax.rsqrt(jnp.mean(hid * hid, axis=1, keepdims=True) + 1e-06)
        normed = (hid * inv_rms * gain_ref[...]).astype(BF)
        grad = grad_ref[...]
        rows_ref[:, :width] = grad
        rows_ref[:, width:] = normed
        half = PARTS // 2
        for part in range(half):
            parts_ref[part * tokens : (part + 1) * tokens, :] = grad[
                :, part * piece : (part + 1) * piece
            ]
            parts_ref[(half + part) * tokens : (half + part + 1) * tokens, :] = normed[
                :, part * piece : (part + 1) * piece
            ]
        slot_ref[...] = routing(ids_ref[...], experts)

    start = pl.multiple_of(step * block_experts, block_experts)
    slot = per_row(slot_ref[pl.ds(start, block_experts), :])
    place = iota(slot.shape, 0) & (SLOTS - 1)
    pick = jnp.where(slot == place.astype(F32), 1.0, 0.0).astype(BF)
    chunk = 1024
    for col in range(0, 2 * width, chunk):
        out_ref[:, col : col + chunk] = dot_nn(pick, rows_ref[:, col : col + chunk]).astype(BF)
    late = slot == (SLOTS + (place >> 2)).astype(F32)
    pick_late = jnp.concatenate(
        [
            jnp.where(late & ((place & (PARTS - 1)) == part), 1.0, 0.0).astype(BF)
            for part in range(PARTS)
        ],
        axis=1,
    )
    out_ref[:, 2 * width :] = dot_nn(pick_late, parts_ref[...]).astype(BF)


def dispatch(ids, grad_out, hidden_in, gain, experts):
    tokens, width = grad_out.shape
    total = 2 * width + 2 * width // PARTS
    steps = 4
    rows = experts * SLOTS
    return kernel_call(
        dispatch_kernel,
        out_shape=jax.ShapeDtypeStruct((rows, total), BF),
        grid=(steps,),
        in_specs=[
            whole(ids.shape),
            whole(grad_out.shape),
            whole(hidden_in.shape),
            whole(gain.shape),
        ],
        out_specs=pl.BlockSpec((rows // steps, total), lambda i: (i, 0)),
        scratch_shapes=[
            pltpu.VMEM((tokens, 2 * width), BF),
            pltpu.VMEM((PARTS * tokens, 2 * width // PARTS), BF),
            pltpu.VMEM((experts, tokens), F32),
        ],
        vmem=16,
        space=None,
        name="dispatch",
    )(ids, grad_out, hidden_in, gain)


def expert_kernel(
    rows_hbm,
    gate_hbm,
    up_hbm,
    down_hbm,
    out_hbm,
    rows_ref,
    gate_ref,
    up_ref,
    down_ref,
    late_ref,
    act_ref,
    out_ref,
    in_sems,
    out_sems,
):
    width, hidden = gate_ref.shape
    rows = rows_ref.shape[0]
    group = rows // 2
    late = group // SLOTS * EXTRA
    quarter = width // PARTS
    chunk = 256

    def fetch(source, target, n):
        copy = pltpu.make_async_copy(source, target, in_sems.at[n])
        copy.start()
        return copy

    def columns(lo, first, last, n):
        at = (slice(lo, lo + group), slice(first, last))
        return fetch(rows_hbm.at[at], rows_ref.at[at], n)

    norm_0 = columns(0, width, 2 * width, 0)
    gate_in = fetch(gate_hbm, gate_ref, 1)
    up_in = fetch(up_hbm, up_ref, 2)
    grad_0 = columns(0, 0, width, 3)
    down_in = fetch(down_hbm, down_ref, 4)
    all_1 = columns(group, 0, 2 * width, 5)
    late_0 = columns(0, 2 * width, 2 * width + 2 * quarter, 6)
    late_1 = columns(group, 2 * width, 2 * width + 2 * quarter, 7)

    def backward(norm, grad, before_up=(), before_grad=(), acts=None):
        gate_pre = dot_nn(norm(), gate_ref[...])
        for copy in before_up:
            copy.wait()
        up_pre = dot_nn(norm(), up_ref[...])
        for copy in before_grad:
            copy.wait()
        score = None
        for col in range(0, hidden, chunk):
            cols = slice(col, col + chunk)
            grad_hid = dot_nt(grad(), down_ref[cols, :])
            gate_part = gate_pre[:, cols]
            sigma = jax.nn.sigmoid(gate_part)
            act = gate_part * sigma
            slope = sigma * (1.0 + gate_part * (1.0 - sigma))
            grad_up = grad_hid * up_pre[:, cols]
            partial = jnp.sum(grad_up * act, axis=1, keepdims=True)
            score = partial if score is None else score + partial
            acts[:, cols] = (grad_up * slope).astype(BF)
            acts[:, hidden + col : hidden + col + chunk] = (grad_hid * act).astype(BF)
        return score

    def pair(acts, cols):
        total = dot_nt(acts[:, :hidden], gate_ref[cols, :])
        return (total + dot_nt(acts[:, hidden:], up_ref[cols, :])).astype(BF)

    sent = []

    def send(lo, height, first, last):
        at = (slice(lo, lo + height), slice(first, last))
        copy = pltpu.make_async_copy(out_ref.at[at], out_hbm.at[at], out_sems.at[len(sent)])
        copy.start()
        sent.append(copy)

    main_scores = []
    for index in range(2):
        at = slice(index * group, (index + 1) * group)
        if index == 0:
            norm_0.wait()
            gate_in.wait()
            waits = ((up_in,), (grad_0, down_in))
        else:
            all_1.wait()
            waits = ((), ())
        acts = act_ref.at[at]
        main_scores.append(
            backward(
                lambda: rows_ref[at, width : 2 * width], lambda: rows_ref[at, :width], *waits, acts
            )
        )
        for col in range(0, width, quarter):
            cols = slice(col, col + quarter)
            out_ref[at, cols] = pair(acts, cols)
        send(index * group, group, 0, width)

    late_0.wait()
    late_1.wait()
    half = group // 2
    few = half // SLOTS * EXTRA
    order = iota((half, half), 0)
    source = (order % few) * PARTS + order // few
    gather = jnp.where(iota((half, half), 1) == source, 1.0, 0.0).astype(BF)
    for block in range(rows // half):
        moved = dot_nn(gather, rows_ref[block * half : (block + 1) * half, 2 * width :]).astype(BF)
        for part in range(PARTS):
            late_ref[block * few : (block + 1) * few, part * 2 * quarter : (part + 1) * 2 * quarter] = (
                moved[part * few : (part + 1) * few]
            )
    acts = act_ref.at[rows:]
    late_score = backward(
        lambda: late_ref[:, width : 2 * width], lambda: late_ref[:, :width], acts=acts
    )
    ends = [pair(acts, slice(col, col + quarter)) for col in range(0, width, quarter)]
    order = iota((half, half), 1)
    scatter = jnp.where(
        iota((half, half), 0) == (order % few) * PARTS + order // few, 1.0, 0.0
    ).astype(BF)
    spread = jnp.where((iota((half, few), 0) >> 2) == iota((half, few), 1), 1.0, 0.0).astype(BF)
    lane = iota((half, LANES), 1)
    for block in range(rows // half):
        at = slice(block * half, (block + 1) * half)
        own = slice(block * few, (block + 1) * few)
        stacked = jnp.concatenate([end[own] for end in ends], axis=0)
        out_ref[at, width : width + quarter] = dot_nn(scatter, stacked).astype(BF)
        spread_score = dot_nn(spread, jnp.broadcast_to(late_score[own], (few, LANES)).astype(BF))
        start = (block % 2) * half
        main_score = main_scores[block // 2][start : start + half]
        out_ref[at, width + quarter :] = jnp.where(
            lane == 0, main_score, jnp.where(lane == 1, spread_score, 0.0)
        ).astype(BF)
    send(0, rows, width, width + quarter + LANES)
    for copy in sent:
        copy.wait()


def expert_backward(arrived, gate_mat, up_mat, down_mat):
    rows = arrived.shape[0]
    width, hidden = gate_mat.shape
    late = rows // SLOTS * EXTRA
    out_shape = (rows, width + width // PARTS + LANES)
    return kernel_call(
        expert_kernel,
        out_shape=jax.ShapeDtypeStruct(out_shape, BF),
        in_specs=[RAW] * 4,
        out_specs=RAW,
        scratch_shapes=[
            pltpu.VMEM(arrived.shape, BF),
            pltpu.VMEM(gate_mat.shape, BF),
            pltpu.VMEM(up_mat.shape, BF),
            pltpu.VMEM(down_mat.shape, BF),
            pltpu.VMEM((late, 2 * width), BF),
            pltpu.VMEM((rows + late, 2 * hidden), BF),
            pltpu.VMEM(out_shape, BF),
            pltpu.SemaphoreType.DMA((8,)),
            pltpu.SemaphoreType.DMA((3,)),
        ],
        vmem=48,
        name="expert",
    )(arrived, gate_mat, up_mat, down_mat)


def placed(ids, rows):
    experts = rows // SLOTS
    slot = per_row(routing(ids, experts))
    place = iota(slot.shape, 0) & (SLOTS - 1)
    return slot == place.astype(F32), slot == (SLOTS + (place >> 2)).astype(F32), place


def plan_kernel(ids_ref, weight_ref, first_ref, late_ref):
    ids = ids_ref[...]
    weights = weight_ref[...]
    top, tokens = ids.shape
    rows = first_ref.shape[1]
    experts = rows // SLOTS
    row = iota((experts, tokens), 0)
    weight = jnp.zeros((experts, tokens), F32)
    for k in range(top):
        weight = weight + jnp.where(ids[k : k + 1, :] == row, weights[k : k + 1, :], 0.0)
    weight = per_row(weight)
    first, late, place = placed(ids, rows)
    high = weight.astype(BF).astype(F32)
    for n, value in enumerate((high, weight - high)):
        first_ref[n * tokens : (n + 1) * tokens, :] = jnp.where(first, value, 0.0).T.astype(BF)
        for part in range(PARTS):
            start = (2 * part + n) * tokens
            hit = late & ((place & (PARTS - 1)) == part)
            late_ref[start : start + tokens, :] = jnp.where(hit, value, 0.0).T.astype(BF)


def plan(ids, weights, experts):
    tokens = ids.shape[1]
    rows = experts * SLOTS
    return kernel_call(
        plan_kernel,
        out_shape=(
            jax.ShapeDtypeStruct((2 * tokens, rows), BF),
            jax.ShapeDtypeStruct((2 * PARTS * tokens, rows), BF),
        ),
        space=pltpu.VMEM,
        vmem=16,
        name="plan",
    )(ids, weights)


def combine_kernel(
    first_ref,
    late_ref,
    grad_ref,
    hid_ref,
    gain_ref,
    back_hbm,
    proj_hbm,
    out_ref,
    attn_ref,
    back_ref,
    proj_ref,
    sems,
):
    tokens, width = grad_ref.shape
    quarter = width // PARTS
    pieces, owners, piece, _ = proj_ref.shape
    group = owners // 8
    heads = attn_ref.shape[1]

    def fetch(source, target, n):
        copy = pltpu.make_async_copy(source, target, sems.at[n])
        copy.start()
        return copy

    backs = []
    for n, part in enumerate((PARTS,) + tuple(range(PARTS))):
        at = (slice(None), slice(part * quarter, (part + 1) * quarter))
        backs.append(fetch(back_hbm.at[at], back_ref.at[at], n))
    def proj_copy(n):
        at = (slice(None), pl.ds(n * group, group))
        return pltpu.make_async_copy(proj_hbm.at[at], proj_ref.at[at], sems.at[len(backs) + n])

    for n in range(8):
        proj_copy(n).start()

    hid = hid_ref[...].astype(F32)
    inv_rms = lax.rsqrt(jnp.mean(hid * hid, axis=1, keepdims=True) + 1e-06)
    backs[0].wait()
    late = dot_nn(late_ref[...], back_ref[:, width:])
    total = jnp.zeros((tokens, 1), F32)
    parts = []
    for part in range(PARTS):
        cols = slice(part * quarter, (part + 1) * quarter)
        backs[1 + part].wait()
        moe = dot_nn(first_ref[...], back_ref[:, cols])
        begin = 2 * part * tokens
        moe = (moe[:tokens] + moe[tokens:]) + (
            late[begin : begin + tokens] + late[begin + tokens : begin + 2 * tokens]
        )
        scaled = moe * gain_ref[:, cols]
        parts.append(scaled)
        total = total + jnp.sum(scaled * (hid[:, cols] * inv_rms), axis=1, keepdims=True)
    inner_mean = total * (1.0 / width)
    for part in range(PARTS):
        cols = slice(part * quarter, (part + 1) * quarter)
        change = parts[part] - hid[:, cols] * inv_rms * inner_mean
        out_ref[:, cols] = (grad_ref[:, cols].astype(F32) + inv_rms * change).astype(BF)

    def project(n, carry):
        proj_copy(n).wait()
        for index in range(group):
            owner = n * group + index
            proj = proj_ref[:, owner].reshape(pieces * piece, width)
            grad = dot_nt(out_ref[...], proj).astype(BF)
            for head in range(heads):
                attn_ref[owner, head] = grad[:, head * HD : (head + 1) * HD]
        return carry

    lax.fori_loop(0, 8, project, 0)


def combine(first, late, grad_out, hidden_in, gain, back, proj):
    tokens, width = grad_out.shape
    pieces, owners, piece, _ = proj.shape
    heads = pieces * piece // HD
    return kernel_call(
        combine_kernel,
        out_shape=(
            jax.ShapeDtypeStruct(grad_out.shape, BF),
            jax.ShapeDtypeStruct((owners, heads, tokens, HD), BF),
        ),
        in_specs=[HELD] * 5 + [RAW] * 2,
        out_specs=(HELD, HELD),
        scratch_shapes=[
            pltpu.VMEM((back.shape[0], width + width // PARTS), BF),
            pltpu.VMEM(proj.shape, BF),
            pltpu.SemaphoreType.DMA((PARTS + 9,)),
        ],
        vmem=50,
        space=None,
        free=(0, 1, 2, 3, 4),
        name="combine",
    )(first, late, grad_out, hidden_in, gain, back, proj)


def score_kernel(ids_ref, score_ref, gate_ref):
    ids = ids_ref[...]
    top, tokens = ids.shape
    rows = score_ref.shape[0]
    experts = rows // SLOTS
    score = score_ref[...].astype(F32)
    first, late, place = placed(ids, rows)
    got = jnp.where(first, score[:, 0:1], 0.0) + jnp.where(
        late & ((place & (PARTS - 1)) == 0), score[:, 1:2], 0.0
    )
    by_expert = jnp.sum(got.reshape(experts, SLOTS, tokens), axis=1)
    row = iota((experts, tokens), 0)
    gates = [
        jnp.sum(jnp.where(ids[k : k + 1, :] == row, by_expert, 0.0), axis=0, keepdims=True)
        for k in range(top)
    ]
    gate_ref[...] = jnp.concatenate(gates, axis=0).astype(BF)


def scores(ids, back):
    rows, total = back.shape
    return kernel_call(
        score_kernel,
        out_shape=jax.ShapeDtypeStruct(ids.shape, BF),
        grid=(1,),
        in_specs=[
            whole(ids.shape),
            pl.BlockSpec((rows, LANES), lambda i: (0, total // LANES - 1)),
        ],
        out_specs=whole(ids.shape),
        vmem=16,
        name="scores",
    )(ids, back)


BLOCK = 256


def probs_kernel(q_ref, k_ref, v_ref, out_ref, mixed_ref):
    length = q_ref.shape[0]
    scale = HD ** (-0.5)
    start = 0
    for lo in range(0, length, BLOCK):
        hi = lo + BLOCK
        scores = dot_nt(k_ref[:hi, :], q_ref[lo:hi, :])
        corner = jnp.where(
            iota((BLOCK, BLOCK), 0) <= iota((BLOCK, BLOCK), 1), scores[lo:], -jnp.inf
        )
        scores = jnp.concatenate([scores[:lo], corner], axis=0) if lo else corner
        peak = jnp.max(scores, axis=0, keepdims=True)
        exp_scores = jnp.exp((scores - peak) * scale)
        total = jnp.sum(exp_scores, axis=0, keepdims=True)
        probs = (exp_scores * (1.0 / total)).astype(BF)
        out_ref[start : start + hi, :] = probs
        mixed_ref[lo:hi, :] = dot_tn(probs, v_ref[:hi, :])
        start += hi


def packed_rows(length):
    return sum(range(BLOCK, length + 1, BLOCK))


def attention_probs(query, key, value):
    tokens, cols = query.shape
    length = tokens // SEQS
    heads = cols // HD
    item = pl.BlockSpec((length, HD), lambda s, h: (s, h))
    rows = packed_rows(length)
    return kernel_call(
        probs_kernel,
        out_shape=(
            jax.ShapeDtypeStruct((SEQS, heads, rows, BLOCK), BF),
            jax.ShapeDtypeStruct(query.shape, F32),
        ),
        grid=(SEQS, heads),
        in_specs=[item] * 3,
        out_specs=(pl.BlockSpec((None, None, rows, BLOCK), lambda s, h: (s, h, 0, 0)), item),
        vmem=20,
        name="probs",
    )(query, key, value)


def attention_kernel(
    probs_ref, mixed_ref, grad_ref, q_ref, k_ref, v_ref, dq_ref, dk_ref, dv_ref, acc_k, acc_v
):
    length = q_ref.shape[0]
    scale = HD ** (-0.5)
    grad_all = grad_ref[...].reshape(length, HD)
    less = -jnp.sum(grad_all.astype(F32) * mixed_ref[...], axis=1, keepdims=True)
    high = less.astype(BF).astype(F32)
    mid = (less - high).astype(BF).astype(F32)
    low = less - high - mid
    lane = iota((length, HD), 1)
    extra = jnp.where(lane == 0, high, jnp.where(lane == 1, mid, jnp.where(lane == 2, low, 0.0)))
    grad_less = jnp.concatenate([grad_all, extra.astype(BF)], axis=1)
    ones = jnp.where(lane < 3, 1.0, 0.0).astype(BF)
    values = jnp.concatenate([v_ref[...], ones], axis=1)
    keys = k_ref[...].T
    starts = [BLOCK * n * (n + 1) // 2 for n in range(length // BLOCK)]

    def score_grads(n):
        hi = (n + 1) * BLOCK
        shifted = dot_nt(values[:hi], grad_less[hi - BLOCK : hi])
        probs = probs_ref[starts[n] : starts[n] + hi, :]
        return (probs.astype(F32) * shifted).astype(BF)

    ready = score_grads(0)
    for n in range(length // BLOCK):
        lo, hi = n * BLOCK, (n + 1) * BLOCK
        grad_scores = ready
        if hi < length:
            ready = score_grads(n + 1)
        dq_ref[lo:hi, :] = (scale * dot_nn(keys[:, :hi], grad_scores)).T.astype(BF)
        dv = dot_nn(probs_ref[starts[n] : starts[n] + hi, :], grad_all[lo:hi])
        dk = dot_nn(grad_scores, q_ref[lo:hi, :])
        if lo:
            acc_k[:lo, :] += dk[:lo]
            acc_v[:lo, :] += dv[:lo]
        acc_k[lo:hi, :] = dk[lo:]
        acc_v[lo:hi, :] = dv[lo:]
    dk_ref[...] = (scale * acc_k[...]).astype(BF)
    dv_ref[...] = acc_v[...].astype(BF)


def attention(probs, mixed, grad_attn, query, key, value):
    tokens, cols = query.shape
    length = tokens // SEQS
    owners, _, part, _ = grad_attn.shape
    item = pl.BlockSpec((length, HD), lambda s, h: (s, h))
    return kernel_call(
        attention_kernel,
        out_shape=[jax.ShapeDtypeStruct(query.shape, BF)] * 3,
        grid=(SEQS, cols // HD),
        in_specs=[
            pl.BlockSpec((None, None) + probs.shape[2:], lambda s, h: (s, h, 0, 0)),
            item,
            pl.BlockSpec((owners // SEQS, None, part, HD), lambda s, h: (s, h, 0, 0)),
            item,
            item,
            item,
        ],
        out_specs=[item] * 3,
        scratch_shapes=[pltpu.VMEM((length, HD), F32), pltpu.VMEM((length, HD), F32)],
        vmem=24,
        free=(2,),
        name="attention",
    )(probs, mixed, grad_attn, query, key, value)


def exchange(rows, experts):
    total = rows.shape[1]
    moved = lax.all_to_all(
        rows.reshape(experts, SLOTS, total),
        ("group", "inner"),
        split_axis=0,
        concat_axis=0,
        tiled=True,
    )
    return moved.reshape(experts * SLOTS, total)


def local(
    grad_out,
    hidden_in,
    norm_gain,
    expert_ids,
    gate_weights,
    gate_proj,
    up_proj,
    down_proj,
    out_proj,
    query_rows,
    key_rows,
    value_rows,
):
    groups = lax.axis_size("group")
    owners = lax.axis_size("inner")
    experts = groups * owners
    gain = norm_gain.reshape(1, -1)
    tokens, width = grad_out.shape
    piece = out_proj.shape[0] // groups
    ids = expert_ids.T
    own_proj = own_rows(lax.axis_index("group").reshape(1), out_proj, groups)
    own_proj, ids, grad_now, hidden_now = lax.optimization_barrier(
        (own_proj, ids, grad_out, hidden_in)
    )
    proj = lax.all_gather(own_proj, ("group", "inner"), axis=0, tiled=False)
    outgoing = dispatch(ids, grad_now, hidden_now, gain, experts)
    arrived = exchange(outgoing, experts)
    answers = expert_backward(arrived, gate_proj[0], up_proj[0], down_proj[0])
    answers, ids_late, query = lax.optimization_barrier((answers, ids, query_rows))
    back = exchange(answers, experts)
    probs, mixed = attention_probs(query, key_rows, value_rows)
    first, late = plan(ids_late, gate_weights.T, experts)
    back, probs, mixed, first, late = lax.optimization_barrier((back, probs, mixed, first, late))
    grad_hidden, grad_attn = combine(
        first, late, grad_out, hidden_in, gain, back, proj.reshape(groups, owners, piece, width)
    )
    heads = grad_attn.shape[1]
    grad_attn, back = lax.optimization_barrier((grad_attn, back))
    grad_gate = scores(ids, back).T
    grad_attn = lax.all_to_all(
        grad_attn.reshape(owners, heads * tokens, HD),
        "inner",
        split_axis=0,
        concat_axis=0,
        tiled=True,
    )
    grad_attn, grad_gate = lax.optimization_barrier((grad_attn, grad_gate))
    grad_q, grad_k, grad_v = attention(
        probs,
        mixed,
        grad_attn.reshape(owners, heads, tokens, HD),
        query_rows,
        key_rows,
        value_rows,
    )
    return (grad_hidden, grad_gate, grad_q, grad_k, grad_v)


def solution(mesh):
    rows = P(("group", "inner"), None)
    stack = P(("group", "inner"), None, None)
    heads = P("group", "inner")
    return jax.shard_map(
        local,
        mesh=mesh,
        in_specs=(
            rows,
            rows,
            P(),
            rows,
            rows,
            stack,
            stack,
            stack,
            P("inner", None),
            heads,
            heads,
            heads,
        ),
        out_specs=(rows, rows, heads, heads, heads),
        check_vma=False,
    )
```

```python
import functools

import jax
import jax.numpy as jnp
from jax import lax
from jax.experimental import pallas as pl
from jax.experimental.pallas import tpu as pltpu
from jax.sharding import PartitionSpec as P

HD = 128
SEQS = 2
SLOTS = 8
EXTRA = 2
PARTS = 4
LANES = 128
BF = jnp.bfloat16
F32 = jnp.float32


def dot_nn(left, right):
    return lax.dot_general(left, right, (((1,), (0,)), ((), ())), preferred_element_type=F32)


def dot_nt(left, right):
    return lax.dot_general(left, right, (((1,), (1,)), ((), ())), preferred_element_type=F32)


def dot_tn(left, right):
    return lax.dot_general(left, right, (((0,), (0,)), ((), ())), preferred_element_type=F32)


HELD = pl.BlockSpec(memory_space=pltpu.VMEM)
RAW = pl.BlockSpec(memory_space=pl.ANY)


def kernel_call(kernel, out_shape, vmem, space=pltpu.HBM, free=(), **fields):
    outs = out_shape
    if space is not None:
        outs = jax.tree.map(lambda out: space(out.shape, out.dtype), out_shape)
    call = pl.pallas_call(
        kernel,
        out_shape=outs,
        compiler_params=pltpu.CompilerParams(vmem_limit_bytes=vmem << 20),
        **fields,
    )
    pin = lambda arg: pltpu.with_memory_space_constraint(arg, pltpu.HBM)
    return lambda *args: call(*[arg if n in free else pin(arg) for n, arg in enumerate(args)])


def whole(shape):
    return pl.BlockSpec(shape, lambda i: (0,) * len(shape))


def iota(shape, dim):
    return lax.broadcasted_iota(jnp.int32, shape, dim)


def routing(ids, experts):
    top, tokens = ids.shape
    row = iota((experts, tokens), 0)
    member = jnp.zeros((experts, tokens), F32)
    for k in range(top):
        member = member + jnp.where(ids[k : k + 1, :] == row, 1.0, 0.0)
    earlier = jnp.where(iota((tokens, tokens), 0) < iota((tokens, tokens), 1), 1.0, 0.0).astype(BF)
    slot = dot_nn(member.astype(BF), earlier)
    return jnp.where(member > 0.5, slot, -1.0)


def per_row(by_expert):
    experts, width = by_expert.shape
    return jnp.broadcast_to(by_expert[:, None, :], (experts, SLOTS, width)).reshape(
        experts * SLOTS, width
    )


def own_rows_kernel(place_ref, proj_ref, own_ref):
    own_ref[...] = proj_ref[...]


def own_rows(place, proj, pieces):
    block = (proj.shape[0] // pieces, proj.shape[1])
    return kernel_call(
        own_rows_kernel,
        out_shape=jax.ShapeDtypeStruct(block, BF),
        grid_spec=pltpu.PrefetchScalarGridSpec(
            num_scalar_prefetch=1,
            grid=(1,),
            in_specs=[pl.BlockSpec(block, lambda i, place: (place[0], 0))],
            out_specs=pl.BlockSpec(block, lambda i, place: (0, 0)),
        ),
        vmem=16,
        free=(0,),
        name="own_rows",
    )(place, proj)


def dispatch_kernel(ids_ref, grad_ref, hid_ref, gain_ref, out_ref, rows_ref, parts_ref, slot_ref):
    tokens, width = grad_ref.shape
    experts = slot_ref.shape[0]
    step = pl.program_id(0)
    block_experts = out_ref.shape[0] // SLOTS
    piece = 2 * width // PARTS

    @pl.when(step == 0)
    def _():
        hid = hid_ref[...].astype(F32)
        inv_rms = lax.rsqrt(jnp.mean(hid * hid, axis=1, keepdims=True) + 1e-06)
        normed = (hid * inv_rms * gain_ref[...]).astype(BF)
        grad = grad_ref[...]
        rows_ref[:, :width] = grad
        rows_ref[:, width:] = normed
        half = PARTS // 2
        for part in range(half):
            parts_ref[part * tokens : (part + 1) * tokens, :] = grad[
                :, part * piece : (part + 1) * piece
            ]
            parts_ref[(half + part) * tokens : (half + part + 1) * tokens, :] = normed[
                :, part * piece : (part + 1) * piece
            ]
        slot_ref[...] = routing(ids_ref[...], experts)

    start = pl.multiple_of(step * block_experts, block_experts)
    slot = per_row(slot_ref[pl.ds(start, block_experts), :])
    place = iota(slot.shape, 0) & (SLOTS - 1)
    pick = jnp.where(slot == place.astype(F32), 1.0, 0.0).astype(BF)
    chunk = 1024
    for col in range(0, 2 * width, chunk):
        out_ref[:, col : col + chunk] = dot_nn(pick, rows_ref[:, col : col + chunk]).astype(BF)
    late = slot == (SLOTS + (place >> 2)).astype(F32)
    pick_late = jnp.concatenate(
        [
            jnp.where(late & ((place & (PARTS - 1)) == part), 1.0, 0.0).astype(BF)
            for part in range(PARTS)
        ],
        axis=1,
    )
    out_ref[:, 2 * width :] = dot_nn(pick_late, parts_ref[...]).astype(BF)


def dispatch(ids, grad_out, hidden_in, gain, experts):
    tokens, width = grad_out.shape
    total = 2 * width + 2 * width // PARTS
    steps = 4
    rows = experts * SLOTS
    return kernel_call(
        dispatch_kernel,
        out_shape=jax.ShapeDtypeStruct((rows, total), BF),
        grid=(steps,),
        in_specs=[
            whole(ids.shape),
            whole(grad_out.shape),
            whole(hidden_in.shape),
            whole(gain.shape),
        ],
        out_specs=pl.BlockSpec((rows // steps, total), lambda i: (i, 0)),
        scratch_shapes=[
            pltpu.VMEM((tokens, 2 * width), BF),
            pltpu.VMEM((PARTS * tokens, 2 * width // PARTS), BF),
            pltpu.VMEM((experts, tokens), F32),
        ],
        vmem=16,
        space=None,
        name="dispatch",
    )(ids, grad_out, hidden_in, gain)


def expert_kernel(
    rows_ref, gate_ref, up_ref, down_ref, out_hbm, late_ref, act_ref, out_ref, out_sems
):
    width, hidden = gate_ref.shape
    rows = rows_ref.shape[0]
    group = rows // 2
    late = group // SLOTS * EXTRA
    quarter = width // PARTS
    chunk = 256

    def backward(norm, grad, acts):
        gate_pre = dot_nn(norm(), gate_ref[...])
        up_pre = dot_nn(norm(), up_ref[...])
        score = None
        for col in range(0, hidden, chunk):
            cols = slice(col, col + chunk)
            grad_hid = dot_nt(grad(), down_ref[cols, :])
            gate_part = gate_pre[:, cols]
            sigma = jax.nn.sigmoid(gate_part)
            act = gate_part * sigma
            slope = sigma * (1.0 + gate_part * (1.0 - sigma))
            grad_up = grad_hid * up_pre[:, cols]
            partial = jnp.sum(grad_up * act, axis=1, keepdims=True)
            score = partial if score is None else score + partial
            acts[:, cols] = (grad_up * slope).astype(BF)
            acts[:, hidden + col : hidden + col + chunk] = (grad_hid * act).astype(BF)
        return score

    def pair(acts, cols):
        total = dot_nt(acts[:, :hidden], gate_ref[cols, :])
        return (total + dot_nt(acts[:, hidden:], up_ref[cols, :])).astype(BF)

    sent = []

    def send(lo, height, first, last):
        at = (slice(lo, lo + height), slice(first, last))
        copy = pltpu.make_async_copy(out_ref.at[at], out_hbm.at[at], out_sems.at[len(sent)])
        copy.start()
        sent.append(copy)

    main_scores = []
    for index in range(2):
        at = slice(index * group, (index + 1) * group)
        acts = act_ref.at[at]
        main_scores.append(
            backward(lambda: rows_ref[at, width : 2 * width], lambda: rows_ref[at, :width], acts)
        )
        for col in range(0, width, quarter):
            cols = slice(col, col + quarter)
            out_ref[at, cols] = pair(acts, cols)
        send(index * group, group, 0, width)

    half = group // 2
    few = half // SLOTS * EXTRA
    order = iota((half, half), 0)
    source = (order % few) * PARTS + order // few
    gather = jnp.where(iota((half, half), 1) == source, 1.0, 0.0).astype(BF)
    for block in range(rows // half):
        moved = dot_nn(gather, rows_ref[block * half : (block + 1) * half, 2 * width :]).astype(BF)
        for part in range(PARTS):
            late_ref[block * few : (block + 1) * few, part * 2 * quarter : (part + 1) * 2 * quarter] = (
                moved[part * few : (part + 1) * few]
            )
    acts = act_ref.at[rows:]
    late_score = backward(
        lambda: late_ref[:, width : 2 * width], lambda: late_ref[:, :width], acts
    )
    ends = [pair(acts, slice(col, col + quarter)) for col in range(0, width, quarter)]
    order = iota((half, half), 1)
    scatter = jnp.where(
        iota((half, half), 0) == (order % few) * PARTS + order // few, 1.0, 0.0
    ).astype(BF)
    spread = jnp.where((iota((half, few), 0) >> 2) == iota((half, few), 1), 1.0, 0.0).astype(BF)
    lane = iota((half, LANES), 1)
    for block in range(rows // half):
        at = slice(block * half, (block + 1) * half)
        own = slice(block * few, (block + 1) * few)
        stacked = jnp.concatenate([end[own] for end in ends], axis=0)
        out_ref[at, width : width + quarter] = dot_nn(scatter, stacked).astype(BF)
        spread_score = dot_nn(spread, jnp.broadcast_to(late_score[own], (few, LANES)).astype(BF))
        start = (block % 2) * half
        main_score = main_scores[block // 2][start : start + half]
        out_ref[at, width + quarter :] = jnp.where(
            lane == 0, main_score, jnp.where(lane == 1, spread_score, 0.0)
        ).astype(BF)
    send(0, rows, width, width + quarter + LANES)
    for copy in sent:
        copy.wait()


def expert_backward(arrived, gate_mat, up_mat, down_mat):
    rows = arrived.shape[0]
    width, hidden = gate_mat.shape
    late = rows // SLOTS * EXTRA
    out_shape = (rows, width + width // PARTS + LANES)
    return kernel_call(
        expert_kernel,
        out_shape=jax.ShapeDtypeStruct(out_shape, BF),
        in_specs=[HELD] * 4,
        out_specs=RAW,
        scratch_shapes=[
            pltpu.VMEM((late, 2 * width), BF),
            pltpu.VMEM((rows + late, 2 * hidden), BF),
            pltpu.VMEM(out_shape, BF),
            pltpu.SemaphoreType.DMA((3,)),
        ],
        vmem=24,
        free=(0, 1, 2, 3),
        name="expert",
    )(arrived, gate_mat, up_mat, down_mat)


def placed(ids, rows):
    experts = rows // SLOTS
    slot = per_row(routing(ids, experts))
    place = iota(slot.shape, 0) & (SLOTS - 1)
    return slot == place.astype(F32), slot == (SLOTS + (place >> 2)).astype(F32), place


def plan_kernel(ids_ref, weight_ref, first_ref, late_ref):
    ids = ids_ref[...]
    weights = weight_ref[...]
    top, tokens = ids.shape
    rows = first_ref.shape[1]
    experts = rows // SLOTS
    row = iota((experts, tokens), 0)
    weight = jnp.zeros((experts, tokens), F32)
    for k in range(top):
        weight = weight + jnp.where(ids[k : k + 1, :] == row, weights[k : k + 1, :], 0.0)
    weight = per_row(weight)
    first, late, place = placed(ids, rows)
    high = weight.astype(BF).astype(F32)
    for n, value in enumerate((high, weight - high)):
        first_ref[n * tokens : (n + 1) * tokens, :] = jnp.where(first, value, 0.0).T.astype(BF)
        for part in range(PARTS):
            start = (2 * part + n) * tokens
            hit = late & ((place & (PARTS - 1)) == part)
            late_ref[start : start + tokens, :] = jnp.where(hit, value, 0.0).T.astype(BF)


def plan(ids, weights, experts):
    tokens = ids.shape[1]
    rows = experts * SLOTS
    return kernel_call(
        plan_kernel,
        out_shape=(
            jax.ShapeDtypeStruct((2 * tokens, rows), BF),
            jax.ShapeDtypeStruct((2 * PARTS * tokens, rows), BF),
        ),
        space=pltpu.VMEM,
        vmem=16,
        name="plan",
    )(ids, weights)


def combine_kernel(
    first_ref,
    late_ref,
    grad_ref,
    hid_ref,
    gain_ref,
    back_hbm,
    proj_hbm,
    out_ref,
    attn_ref,
    back_ref,
    proj_ref,
    sems,
):
    tokens, width = grad_ref.shape
    quarter = width // PARTS
    pieces, owners, piece, _ = proj_ref.shape
    group = owners // 8
    heads = attn_ref.shape[1]

    def fetch(source, target, n):
        copy = pltpu.make_async_copy(source, target, sems.at[n])
        copy.start()
        return copy

    backs = []
    for n, part in enumerate((PARTS,) + tuple(range(PARTS))):
        at = (slice(None), slice(part * quarter, (part + 1) * quarter))
        backs.append(fetch(back_hbm.at[at], back_ref.at[at], n))
    def proj_copy(n):
        at = (slice(None), pl.ds(n * group, group))
        return pltpu.make_async_copy(proj_hbm.at[at], proj_ref.at[at], sems.at[len(backs) + n])

    for n in range(8):
        proj_copy(n).start()

    hid = hid_ref[...].astype(F32)
    inv_rms = lax.rsqrt(jnp.mean(hid * hid, axis=1, keepdims=True) + 1e-06)
    backs[0].wait()
    late = dot_nn(late_ref[...], back_ref[:, width:])
    total = jnp.zeros((tokens, 1), F32)
    parts = []
    for part in range(PARTS):
        cols = slice(part * quarter, (part + 1) * quarter)
        backs[1 + part].wait()
        moe = dot_nn(first_ref[...], back_ref[:, cols])
        begin = 2 * part * tokens
        moe = (moe[:tokens] + moe[tokens:]) + (
            late[begin : begin + tokens] + late[begin + tokens : begin + 2 * tokens]
        )
        scaled = moe * gain_ref[:, cols]
        parts.append(scaled)
        total = total + jnp.sum(scaled * (hid[:, cols] * inv_rms), axis=1, keepdims=True)
    inner_mean = total * (1.0 / width)
    for part in range(PARTS):
        cols = slice(part * quarter, (part + 1) * quarter)
        change = parts[part] - hid[:, cols] * inv_rms * inner_mean
        out_ref[:, cols] = (grad_ref[:, cols].astype(F32) + inv_rms * change).astype(BF)

    def project(n, carry):
        proj_copy(n).wait()
        for index in range(group):
            owner = n * group + index
            proj = proj_ref[:, owner].reshape(pieces * piece, width)
            grad = dot_nt(out_ref[...], proj).astype(BF)
            for head in range(heads):
                attn_ref[owner, head] = grad[:, head * HD : (head + 1) * HD]
        return carry

    lax.fori_loop(0, 8, project, 0)


def combine(first, late, grad_out, hidden_in, gain, back, proj):
    tokens, width = grad_out.shape
    pieces, owners, piece, _ = proj.shape
    heads = pieces * piece // HD
    return kernel_call(
        combine_kernel,
        out_shape=(
            jax.ShapeDtypeStruct(grad_out.shape, BF),
            jax.ShapeDtypeStruct((owners, heads, tokens, HD), BF),
        ),
        in_specs=[HELD] * 5 + [RAW] * 2,
        out_specs=(HELD, HELD),
        scratch_shapes=[
            pltpu.VMEM((back.shape[0], width + width // PARTS), BF),
            pltpu.VMEM(proj.shape, BF),
            pltpu.SemaphoreType.DMA((PARTS + 9,)),
        ],
        vmem=50,
        space=None,
        free=(0, 1, 2, 3, 4),
        name="combine",
    )(first, late, grad_out, hidden_in, gain, back, proj)


def score_kernel(ids_ref, score_ref, gate_ref):
    ids = ids_ref[...]
    top, tokens = ids.shape
    rows = score_ref.shape[0]
    experts = rows // SLOTS
    score = score_ref[...].astype(F32)
    first, late, place = placed(ids, rows)
    got = jnp.where(first, score[:, 0:1], 0.0) + jnp.where(
        late & ((place & (PARTS - 1)) == 0), score[:, 1:2], 0.0
    )
    by_expert = jnp.sum(got.reshape(experts, SLOTS, tokens), axis=1)
    row = iota((experts, tokens), 0)
    gates = [
        jnp.sum(jnp.where(ids[k : k + 1, :] == row, by_expert, 0.0), axis=0, keepdims=True)
        for k in range(top)
    ]
    gate_ref[...] = jnp.concatenate(gates, axis=0).astype(BF)


def scores(ids, back):
    rows, total = back.shape
    return kernel_call(
        score_kernel,
        out_shape=jax.ShapeDtypeStruct(ids.shape, BF),
        grid=(1,),
        in_specs=[
            whole(ids.shape),
            pl.BlockSpec((rows, LANES), lambda i: (0, total // LANES - 1)),
        ],
        out_specs=whole(ids.shape),
        vmem=16,
        name="scores",
    )(ids, back)


BLOCK = 256


def probs_kernel(q_ref, k_ref, v_ref, out_ref, mixed_ref):
    length = q_ref.shape[0]
    scale = HD ** (-0.5)
    start = 0
    for lo in range(0, length, BLOCK):
        hi = lo + BLOCK
        scores = dot_nt(k_ref[:hi, :], q_ref[lo:hi, :])
        corner = jnp.where(
            iota((BLOCK, BLOCK), 0) <= iota((BLOCK, BLOCK), 1), scores[lo:], -jnp.inf
        )
        scores = jnp.concatenate([scores[:lo], corner], axis=0) if lo else corner
        peak = jnp.max(scores, axis=0, keepdims=True)
        exp_scores = jnp.exp((scores - peak) * scale)
        total = jnp.sum(exp_scores, axis=0, keepdims=True)
        probs = (exp_scores * (1.0 / total)).astype(BF)
        out_ref[start : start + hi, :] = probs
        mixed_ref[lo:hi, :] = dot_tn(probs, v_ref[:hi, :])
        start += hi


def packed_rows(length):
    return sum(range(BLOCK, length + 1, BLOCK))


def attention_probs(query, key, value):
    tokens, cols = query.shape
    length = tokens // SEQS
    heads = cols // HD
    item = pl.BlockSpec((length, HD), lambda s, h: (s, h))
    rows = packed_rows(length)
    return kernel_call(
        probs_kernel,
        out_shape=(
            jax.ShapeDtypeStruct((SEQS, heads, rows, BLOCK), BF),
            jax.ShapeDtypeStruct(query.shape, F32),
        ),
        grid=(SEQS, heads),
        in_specs=[item] * 3,
        out_specs=(pl.BlockSpec((None, None, rows, BLOCK), lambda s, h: (s, h, 0, 0)), item),
        vmem=20,
        name="probs",
    )(query, key, value)


def attention_kernel(
    probs_ref, mixed_ref, grad_ref, q_ref, k_ref, v_ref, dq_ref, dk_ref, dv_ref, acc_k, acc_v
):
    length = q_ref.shape[0]
    scale = HD ** (-0.5)
    grad_all = grad_ref[...].reshape(length, HD)
    less = -jnp.sum(grad_all.astype(F32) * mixed_ref[...], axis=1, keepdims=True)
    high = less.astype(BF).astype(F32)
    mid = (less - high).astype(BF).astype(F32)
    low = less - high - mid
    lane = iota((length, HD), 1)
    extra = jnp.where(lane == 0, high, jnp.where(lane == 1, mid, jnp.where(lane == 2, low, 0.0)))
    grad_less = jnp.concatenate([grad_all, extra.astype(BF)], axis=1)
    ones = jnp.where(lane < 3, 1.0, 0.0).astype(BF)
    values = jnp.concatenate([v_ref[...], ones], axis=1)
    keys = k_ref[...].T
    starts = [BLOCK * n * (n + 1) // 2 for n in range(length // BLOCK)]

    def score_grads(n):
        hi = (n + 1) * BLOCK
        shifted = dot_nt(values[:hi], grad_less[hi - BLOCK : hi])
        probs = probs_ref[starts[n] : starts[n] + hi, :]
        return (probs.astype(F32) * shifted).astype(BF)

    ready = score_grads(0)
    for n in range(length // BLOCK):
        lo, hi = n * BLOCK, (n + 1) * BLOCK
        grad_scores = ready
        if hi < length:
            ready = score_grads(n + 1)
        dq_ref[lo:hi, :] = (scale * dot_nn(keys[:, :hi], grad_scores)).T.astype(BF)
        dv = dot_nn(probs_ref[starts[n] : starts[n] + hi, :], grad_all[lo:hi])
        dk = dot_nn(grad_scores, q_ref[lo:hi, :])
        if lo:
            acc_k[:lo, :] += dk[:lo]
            acc_v[:lo, :] += dv[:lo]
        acc_k[lo:hi, :] = dk[lo:]
        acc_v[lo:hi, :] = dv[lo:]
    dk_ref[...] = (scale * acc_k[...]).astype(BF)
    dv_ref[...] = acc_v[...].astype(BF)


def attention(probs, mixed, grad_attn, query, key, value):
    tokens, cols = query.shape
    length = tokens // SEQS
    owners, _, part, _ = grad_attn.shape
    item = pl.BlockSpec((length, HD), lambda s, h: (s, h))
    return kernel_call(
        attention_kernel,
        out_shape=[jax.ShapeDtypeStruct(query.shape, BF)] * 3,
        grid=(SEQS, cols // HD),
        in_specs=[
            pl.BlockSpec((None, None) + probs.shape[2:], lambda s, h: (s, h, 0, 0)),
            item,
            pl.BlockSpec((owners // SEQS, None, part, HD), lambda s, h: (s, h, 0, 0)),
            item,
            item,
            item,
        ],
        out_specs=[item] * 3,
        scratch_shapes=[pltpu.VMEM((length, HD), F32), pltpu.VMEM((length, HD), F32)],
        vmem=24,
        free=(2,),
        name="attention",
    )(probs, mixed, grad_attn, query, key, value)


def exchange(rows, experts):
    total = rows.shape[1]
    moved = lax.all_to_all(
        rows.reshape(experts, SLOTS, total),
        ("group", "inner"),
        split_axis=0,
        concat_axis=0,
        tiled=True,
    )
    return moved.reshape(experts * SLOTS, total)


def local(
    grad_out,
    hidden_in,
    norm_gain,
    expert_ids,
    gate_weights,
    gate_proj,
    up_proj,
    down_proj,
    out_proj,
    query_rows,
    key_rows,
    value_rows,
):
    groups = lax.axis_size("group")
    owners = lax.axis_size("inner")
    experts = groups * owners
    gain = norm_gain.reshape(1, -1)
    tokens, width = grad_out.shape
    piece = out_proj.shape[0] // groups
    ids = expert_ids.T
    own_proj = own_rows(lax.axis_index("group").reshape(1), out_proj, groups)
    own_proj, ids, grad_now, hidden_now = lax.optimization_barrier(
        (own_proj, ids, grad_out, hidden_in)
    )
    proj = lax.all_gather(own_proj, ("group", "inner"), axis=0, tiled=False)
    outgoing = dispatch(ids, grad_now, hidden_now, gain, experts)
    arrived = exchange(outgoing, experts)
    answers = expert_backward(arrived, gate_proj[0], up_proj[0], down_proj[0])
    answers, ids_late, query = lax.optimization_barrier((answers, ids, query_rows))
    back = exchange(answers, experts)
    probs, mixed = attention_probs(query, key_rows, value_rows)
    first, late = plan(ids_late, gate_weights.T, experts)
    back, probs, mixed, first, late = lax.optimization_barrier((back, probs, mixed, first, late))
    grad_hidden, grad_attn = combine(
        first, late, grad_out, hidden_in, gain, back, proj.reshape(groups, owners, piece, width)
    )
    heads = grad_attn.shape[1]
    grad_attn, back = lax.optimization_barrier((grad_attn, back))
    grad_gate = scores(ids, back).T
    grad_attn = lax.all_to_all(
        grad_attn.reshape(owners, heads * tokens, HD),
        "inner",
        split_axis=0,
        concat_axis=0,
        tiled=True,
    )
    grad_attn, grad_gate = lax.optimization_barrier((grad_attn, grad_gate))
    grad_q, grad_k, grad_v = attention(
        probs,
        mixed,
        grad_attn.reshape(owners, heads, tokens, HD),
        query_rows,
        key_rows,
        value_rows,
    )
    return (grad_hidden, grad_gate, grad_q, grad_k, grad_v)


def solution(mesh):
    rows = P(("group", "inner"), None)
    stack = P(("group", "inner"), None, None)
    heads = P("group", "inner")
    return jax.shard_map(
        local,
        mesh=mesh,
        in_specs=(
            rows,
            rows,
            P(),
            rows,
            rows,
            stack,
            stack,
            stack,
            P("inner", None),
            heads,
            heads,
            heads,
        ),
        out_specs=(rows, rows, heads, heads, heads),
        check_vma=False,
    )
```

```python
import functools

import jax
import jax.numpy as jnp
from jax import lax
from jax.experimental import pallas as pl
from jax.experimental.pallas import tpu as pltpu
from jax.sharding import PartitionSpec as P

HD = 128
SEQS = 2
SLOTS = 8
EXTRA = 2
PARTS = 4
PLACES = 16
BF = jnp.bfloat16
F32 = jnp.float32


def dot_nn(left, right):
    return lax.dot_general(left, right, (((1,), (0,)), ((), ())), preferred_element_type=F32)


def dot_nt(left, right):
    return lax.dot_general(left, right, (((1,), (1,)), ((), ())), preferred_element_type=F32)


def dot_tn(left, right):
    return lax.dot_general(left, right, (((0,), (0,)), ((), ())), preferred_element_type=F32)


HELD = pl.BlockSpec(memory_space=pltpu.VMEM)
RAW = pl.BlockSpec(memory_space=pl.ANY)


def kernel_call(kernel, out_shape, vmem, space=pltpu.HBM, free=(), **fields):
    outs = out_shape
    if space is not None:
        outs = jax.tree.map(lambda out: space(out.shape, out.dtype), out_shape)
    call = pl.pallas_call(
        kernel,
        out_shape=outs,
        compiler_params=pltpu.CompilerParams(vmem_limit_bytes=vmem << 20),
        **fields,
    )
    pin = lambda arg: pltpu.with_memory_space_constraint(arg, pltpu.HBM)
    return lambda *args: call(*[arg if n in free else pin(arg) for n, arg in enumerate(args)])


def whole(shape):
    return pl.BlockSpec(shape, lambda i: (0,) * len(shape))


def iota(shape, dim):
    return lax.broadcasted_iota(jnp.int32, shape, dim)


def routing(ids, experts):
    top, tokens = ids.shape
    row = iota((experts, tokens), 0)
    member = jnp.zeros((experts, tokens), F32)
    for k in range(top):
        member = member + jnp.where(ids[k : k + 1, :] == row, 1.0, 0.0)
    earlier = jnp.where(iota((tokens, tokens), 0) < iota((tokens, tokens), 1), 1.0, 0.0).astype(BF)
    slot = dot_nn(member.astype(BF), earlier)
    return jnp.where(member > 0.5, slot, -1.0)


def per_row(by_expert, count=SLOTS):
    experts, width = by_expert.shape
    return jnp.broadcast_to(by_expert[:, None, :], (experts, count, width)).reshape(
        experts * count, width
    )


def own_rows_kernel(place_ref, proj_ref, own_ref):
    own_ref[...] = proj_ref[...]


def own_rows(place, proj, pieces):
    block = (proj.shape[0] // pieces, proj.shape[1])
    return kernel_call(
        own_rows_kernel,
        out_shape=jax.ShapeDtypeStruct(block, BF),
        grid_spec=pltpu.PrefetchScalarGridSpec(
            num_scalar_prefetch=1,
            grid=(1,),
            in_specs=[pl.BlockSpec(block, lambda i, place: (place[0], 0))],
            out_specs=pl.BlockSpec(block, lambda i, place: (0, 0)),
        ),
        vmem=16,
        free=(0,),
        name="own_rows",
    )(place, proj)


def dispatch_kernel(ids_ref, grad_ref, hid_ref, gain_ref, out_ref, rows_ref, parts_ref, slot_ref):
    tokens, width = grad_ref.shape
    experts = slot_ref.shape[0]
    step = pl.program_id(0)
    block_experts = out_ref.shape[0] // SLOTS
    piece = 2 * width // PARTS

    @pl.when(step == 0)
    def _():
        hid = hid_ref[...].astype(F32)
        inv_rms = lax.rsqrt(jnp.mean(hid * hid, axis=1, keepdims=True) + 1e-06)
        normed = (hid * inv_rms * gain_ref[...]).astype(BF)
        grad = grad_ref[...]
        rows_ref[:, :width] = grad
        rows_ref[:, width:] = normed
        half = PARTS // 2
        for part in range(half):
            parts_ref[part * tokens : (part + 1) * tokens, :] = grad[
                :, part * piece : (part + 1) * piece
            ]
            parts_ref[(half + part) * tokens : (half + part + 1) * tokens, :] = normed[
                :, part * piece : (part + 1) * piece
            ]
        slot_ref[...] = routing(ids_ref[...], experts)

    start = pl.multiple_of(step * block_experts, block_experts)
    slot = per_row(slot_ref[pl.ds(start, block_experts), :])
    place = iota(slot.shape, 0) & (SLOTS - 1)
    pick = jnp.where(slot == place.astype(F32), 1.0, 0.0).astype(BF)
    chunk = 1024
    for col in range(0, 2 * width, chunk):
        out_ref[:, col : col + chunk] = dot_nn(pick, rows_ref[:, col : col + chunk]).astype(BF)
    late = slot == (SLOTS + (place >> 2)).astype(F32)
    pick_late = jnp.concatenate(
        [
            jnp.where(late & ((place & (PARTS - 1)) == part), 1.0, 0.0).astype(BF)
            for part in range(PARTS)
        ],
        axis=1,
    )
    out_ref[:, 2 * width :] = dot_nn(pick_late, parts_ref[...]).astype(BF)


def dispatch(ids, grad_out, hidden_in, gain, experts):
    tokens, width = grad_out.shape
    total = 2 * width + 2 * width // PARTS
    steps = 4
    rows = experts * SLOTS
    return kernel_call(
        dispatch_kernel,
        out_shape=jax.ShapeDtypeStruct((rows, total), BF),
        grid=(steps,),
        in_specs=[
            whole(ids.shape),
            whole(grad_out.shape),
            whole(hidden_in.shape),
            whole(gain.shape),
        ],
        out_specs=pl.BlockSpec((rows // steps, total), lambda i: (i, 0)),
        scratch_shapes=[
            pltpu.VMEM((tokens, 2 * width), BF),
            pltpu.VMEM((PARTS * tokens, 2 * width // PARTS), BF),
            pltpu.VMEM((experts, tokens), F32),
        ],
        vmem=16,
        space=None,
        name="dispatch",
    )(ids, grad_out, hidden_in, gain)


def expert_kernel(
    rows_ref, gate_ref, up_ref, down_ref, out_hbm, score_ref, late_ref, act_ref, out_ref, out_sems
):
    width, hidden = gate_ref.shape
    rows = rows_ref.shape[0]
    group = rows // 2
    late = group // SLOTS * EXTRA
    quarter = width // PARTS
    chunk = 256

    def backward(norm, grad, acts):
        gate_pre = dot_nn(norm(), gate_ref[...])
        up_pre = dot_nn(norm(), up_ref[...])
        score = None
        for col in range(0, hidden, chunk):
            cols = slice(col, col + chunk)
            grad_hid = dot_nt(grad(), down_ref[cols, :])
            gate_part = gate_pre[:, cols]
            sigma = jax.nn.sigmoid(gate_part)
            act = gate_part * sigma
            slope = sigma * (1.0 + gate_part * (1.0 - sigma))
            grad_up = grad_hid * up_pre[:, cols]
            partial = jnp.sum(grad_up * act, axis=1, keepdims=True)
            score = partial if score is None else score + partial
            acts[:, cols] = (grad_up * slope).astype(BF)
            acts[:, hidden + col : hidden + col + chunk] = (grad_hid * act).astype(BF)
        return score

    def pair(acts, cols):
        total = dot_nt(acts[:, :hidden], gate_ref[cols, :])
        return (total + dot_nt(acts[:, hidden:], up_ref[cols, :])).astype(BF)

    sent = []

    def send(lo, height, first, last):
        at = (slice(lo, lo + height), slice(first, last))
        copy = pltpu.make_async_copy(out_ref.at[at], out_hbm.at[at], out_sems.at[len(sent)])
        copy.start()
        sent.append(copy)

    main_scores = []
    for index in range(2):
        at = slice(index * group, (index + 1) * group)
        acts = act_ref.at[at]
        main_scores.append(
            backward(lambda: rows_ref[at, width : 2 * width], lambda: rows_ref[at, :width], acts)
        )
        for col in range(0, width, quarter):
            cols = slice(col, col + quarter)
            out_ref[at, cols] = pair(acts, cols)
        send(index * group, group, 0, width)

    half = group // 2
    few = half // SLOTS * EXTRA
    order = iota((half, half), 0)
    source = (order % few) * PARTS + order // few
    gather = jnp.where(iota((half, half), 1) == source, 1.0, 0.0).astype(BF)
    for block in range(rows // half):
        moved = dot_nn(gather, rows_ref[block * half : (block + 1) * half, 2 * width :]).astype(BF)
        for part in range(PARTS):
            late_ref[block * few : (block + 1) * few, part * 2 * quarter : (part + 1) * 2 * quarter] = (
                moved[part * few : (part + 1) * few]
            )
    acts = act_ref.at[rows:]
    late_score = backward(
        lambda: late_ref[:, width : 2 * width], lambda: late_ref[:, :width], acts
    )
    ends = [pair(acts, slice(col, col + quarter)) for col in range(0, width, quarter)]
    order = iota((half, half), 1)
    scatter = jnp.where(
        iota((half, half), 0) == (order % few) * PARTS + order // few, 1.0, 0.0
    ).astype(BF)
    for block in range(rows // half):
        at = slice(block * half, (block + 1) * half)
        own = slice(block * few, (block + 1) * few)
        stacked = jnp.concatenate([end[own] for end in ends], axis=0)
        out_ref[at, width : width + quarter] = dot_nn(scatter, stacked).astype(BF)
    send(0, rows, width, width + quarter)

    def by_source(score, count, base):
        height = score.shape[0]
        sources = score_ref.shape[1]
        place = base + (iota((height, PLACES), 0) & (count - 1))
        values = jnp.where(place == iota((height, PLACES), 1), score, 0.0).astype(BF)
        source = iota((height, sources), 0) // count == iota((height, sources), 1)
        return dot_tn(values, jnp.where(source, 1.0, 0.0).astype(BF))

    scores_main = by_source(jnp.concatenate(main_scores, axis=0), SLOTS, 0)
    score_ref[...] = (scores_main + by_source(late_score, EXTRA, SLOTS)).astype(BF)
    for copy in sent:
        copy.wait()


def expert_backward(arrived, gate_mat, up_mat, down_mat):
    rows = arrived.shape[0]
    width, hidden = gate_mat.shape
    late = rows // SLOTS * EXTRA
    out_shape = (rows, width + width // PARTS)
    return kernel_call(
        expert_kernel,
        out_shape=(
            jax.ShapeDtypeStruct(out_shape, BF),
            jax.ShapeDtypeStruct((PLACES, rows // SLOTS), BF),
        ),
        in_specs=[HELD] * 4,
        out_specs=(RAW, pl.BlockSpec((PLACES, rows // SLOTS), lambda: (0, 0))),
        scratch_shapes=[
            pltpu.VMEM((late, 2 * width), BF),
            pltpu.VMEM((rows + late, 2 * hidden), BF),
            pltpu.VMEM(out_shape, BF),
            pltpu.SemaphoreType.DMA((3,)),
        ],
        vmem=24,
        free=(0, 1, 2, 3),
        name="expert",
    )(arrived, gate_mat, up_mat, down_mat)


def placed(ids, rows):
    experts = rows // SLOTS
    slot = per_row(routing(ids, experts))
    place = iota(slot.shape, 0) & (SLOTS - 1)
    return slot == place.astype(F32), slot == (SLOTS + (place >> 2)).astype(F32), place


def plan_kernel(ids_ref, weight_ref, first_ref, late_ref):
    ids = ids_ref[...]
    weights = weight_ref[...]
    top, tokens = ids.shape
    rows = first_ref.shape[1]
    experts = rows // SLOTS
    row = iota((experts, tokens), 0)
    weight = jnp.zeros((experts, tokens), F32)
    for k in range(top):
        weight = weight + jnp.where(ids[k : k + 1, :] == row, weights[k : k + 1, :], 0.0)
    weight = per_row(weight)
    first, late, place = placed(ids, rows)
    high = weight.astype(BF).astype(F32)
    for n, value in enumerate((high, weight - high)):
        first_ref[n * tokens : (n + 1) * tokens, :] = jnp.where(first, value, 0.0).T.astype(BF)
        for part in range(PARTS):
            start = (2 * part + n) * tokens
            hit = late & ((place & (PARTS - 1)) == part)
            late_ref[start : start + tokens, :] = jnp.where(hit, value, 0.0).T.astype(BF)


def plan(ids, weights, experts):
    tokens = ids.shape[1]
    rows = experts * SLOTS
    return kernel_call(
        plan_kernel,
        out_shape=(
            jax.ShapeDtypeStruct((2 * tokens, rows), BF),
            jax.ShapeDtypeStruct((2 * PARTS * tokens, rows), BF),
        ),
        space=pltpu.VMEM,
        vmem=16,
        name="plan",
    )(ids, weights)


def combine_kernel(
    first_ref,
    late_hbm,
    grad_ref,
    hid_ref,
    gain_ref,
    back_hbm,
    proj_hbm,
    out_ref,
    attn_ref,
    back_ref,
    proj_ref,
    late_ref,
    sems,
):
    tokens, width = grad_ref.shape
    quarter = width // PARTS
    pieces, owners, piece, _ = proj_ref.shape
    group = owners // 8
    heads = attn_ref.shape[1]

    def fetch(source, target, n):
        copy = pltpu.make_async_copy(source, target, sems.at[n])
        copy.start()
        return copy

    late_in = fetch(late_hbm, late_ref, PARTS + 9)
    backs = []
    for n, part in enumerate((PARTS,) + tuple(range(PARTS))):
        at = (slice(None), slice(part * quarter, (part + 1) * quarter))
        backs.append(fetch(back_hbm.at[at], back_ref.at[at], n))
    def proj_copy(n):
        at = (slice(None), pl.ds(n * group, group))
        return pltpu.make_async_copy(proj_hbm.at[at], proj_ref.at[at], sems.at[len(backs) + n])

    for n in range(8):
        proj_copy(n).start()

    hid = hid_ref[...].astype(F32)
    inv_rms = lax.rsqrt(jnp.mean(hid * hid, axis=1, keepdims=True) + 1e-06)
    late_in.wait()
    backs[0].wait()
    late = dot_nn(late_ref[...], back_ref[:, width:])
    total = jnp.zeros((tokens, 1), F32)
    parts = []
    for part in range(PARTS):
        cols = slice(part * quarter, (part + 1) * quarter)
        backs[1 + part].wait()
        moe = dot_nn(first_ref[...], back_ref[:, cols])
        begin = 2 * part * tokens
        moe = (moe[:tokens] + moe[tokens:]) + (
            late[begin : begin + tokens] + late[begin + tokens : begin + 2 * tokens]
        )
        scaled = moe * gain_ref[:, cols]
        parts.append(scaled)
        total = total + jnp.sum(scaled * (hid[:, cols] * inv_rms), axis=1, keepdims=True)
    inner_mean = total * (1.0 / width)
    for part in range(PARTS):
        cols = slice(part * quarter, (part + 1) * quarter)
        change = parts[part] - hid[:, cols] * inv_rms * inner_mean
        out_ref[:, cols] = (grad_ref[:, cols].astype(F32) + inv_rms * change).astype(BF)

    def project(n, carry):
        proj_copy(n).wait()
        for index in range(group):
            owner = n * group + index
            proj = proj_ref[:, owner].reshape(pieces * piece, width)
            grad = dot_nt(out_ref[...], proj).astype(BF)
            for head in range(heads):
                attn_ref[owner, head] = grad[:, head * HD : (head + 1) * HD]
        return carry

    lax.fori_loop(0, 8, project, 0)


def combine(first, late, grad_out, hidden_in, gain, back, proj):
    tokens, width = grad_out.shape
    pieces, owners, piece, _ = proj.shape
    heads = pieces * piece // HD
    return kernel_call(
        combine_kernel,
        out_shape=(
            jax.ShapeDtypeStruct(grad_out.shape, BF),
            jax.ShapeDtypeStruct((owners, heads, tokens, HD), BF),
        ),
        in_specs=[HELD, RAW] + [HELD] * 3 + [RAW] * 2,
        out_specs=(HELD, HELD),
        scratch_shapes=[
            pltpu.VMEM((back.shape[0], width + width // PARTS), BF),
            pltpu.VMEM(proj.shape, BF),
            pltpu.VMEM(late.shape, BF),
            pltpu.SemaphoreType.DMA((PARTS + 10,)),
        ],
        vmem=50,
        space=None,
        free=(0, 1, 2, 3, 4),
        name="combine",
    )(first, late, grad_out, hidden_in, gain, back, proj)


def score_kernel(me_ref, ids_ref, score_ref, gate_ref):
    ids = ids_ref[...]
    top, tokens = ids.shape
    rows, devices = score_ref.shape
    experts = rows // PLACES
    mine = iota((rows, devices), 1) == me_ref[0]
    score = jnp.sum(jnp.where(mine, score_ref[...].astype(F32), 0.0), axis=1, keepdims=True)
    slot = per_row(routing(ids, experts), PLACES)
    place = iota(slot.shape, 0) & (PLACES - 1)
    got = jnp.where(slot == place.astype(F32), score, 0.0)
    by_expert = jnp.sum(got.reshape(experts, PLACES, tokens), axis=1)
    row = iota((experts, tokens), 0)
    gates = [
        jnp.sum(jnp.where(ids[k : k + 1, :] == row, by_expert, 0.0), axis=0, keepdims=True)
        for k in range(top)
    ]
    gate_ref[...] = jnp.concatenate(gates, axis=0).astype(BF)


def scores(me, ids, gathered):
    return kernel_call(
        score_kernel,
        out_shape=jax.ShapeDtypeStruct(ids.shape, BF),
        grid=(1,),
        in_specs=[
            pl.BlockSpec(memory_space=pltpu.SMEM),
            whole(ids.shape),
            whole(gathered.shape),
        ],
        out_specs=whole(ids.shape),
        vmem=16,
        free=(0,),
        name="scores",
    )(me, ids, gathered)


BLOCK = 256


def probs_kernel(q_ref, k_ref, v_ref, out_ref, mixed_ref):
    length = q_ref.shape[0]
    scale = HD ** (-0.5)
    start = 0
    for lo in range(0, length, BLOCK):
        hi = lo + BLOCK
        scores = dot_nt(k_ref[:hi, :], q_ref[lo:hi, :])
        corner = jnp.where(
            iota((BLOCK, BLOCK), 0) <= iota((BLOCK, BLOCK), 1), scores[lo:], -jnp.inf
        )
        scores = jnp.concatenate([scores[:lo], corner], axis=0) if lo else corner
        peak = jnp.max(scores, axis=0, keepdims=True)
        exp_scores = jnp.exp((scores - peak) * scale)
        total = jnp.sum(exp_scores, axis=0, keepdims=True)
        probs = (exp_scores * (1.0 / total)).astype(BF)
        out_ref[start : start + hi, :] = probs
        mixed_ref[lo:hi, :] = dot_tn(probs, v_ref[:hi, :])
        start += hi


def packed_rows(length):
    return sum(range(BLOCK, length + 1, BLOCK))


def attention_probs(query, key, value):
    tokens, cols = query.shape
    length = tokens // SEQS
    heads = cols // HD
    item = pl.BlockSpec((length, HD), lambda s, h: (s, h))
    rows = packed_rows(length)
    return kernel_call(
        probs_kernel,
        out_shape=(
            jax.ShapeDtypeStruct((SEQS, heads, rows, BLOCK), BF),
            jax.ShapeDtypeStruct(query.shape, F32),
        ),
        grid=(SEQS, heads),
        in_specs=[item] * 3,
        out_specs=(pl.BlockSpec((None, None, rows, BLOCK), lambda s, h: (s, h, 0, 0)), item),
        vmem=20,
        name="probs",
    )(query, key, value)


def attention_kernel(
    probs_ref, mixed_ref, grad_ref, q_ref, k_ref, v_ref, dq_ref, dk_ref, dv_ref, acc_k, acc_v
):
    length = q_ref.shape[0]
    scale = HD ** (-0.5)
    grad_all = grad_ref[...].reshape(length, HD)
    less = -jnp.sum(grad_all.astype(F32) * mixed_ref[...], axis=1, keepdims=True)
    high = less.astype(BF).astype(F32)
    mid = (less - high).astype(BF).astype(F32)
    low = less - high - mid
    lane = iota((length, HD), 1)
    extra = jnp.where(lane == 0, high, jnp.where(lane == 1, mid, jnp.where(lane == 2, low, 0.0)))
    grad_less = jnp.concatenate([grad_all, extra.astype(BF)], axis=1)
    ones = jnp.where(lane < 3, 1.0, 0.0).astype(BF)
    values = jnp.concatenate([v_ref[...], ones], axis=1)
    keys = k_ref[...].T
    starts = [BLOCK * n * (n + 1) // 2 for n in range(length // BLOCK)]

    def score_grads(n):
        hi = (n + 1) * BLOCK
        shifted = dot_nt(values[:hi], grad_less[hi - BLOCK : hi])
        probs = probs_ref[starts[n] : starts[n] + hi, :]
        return (probs.astype(F32) * shifted).astype(BF)

    ready = score_grads(0)
    for n in range(length // BLOCK):
        lo, hi = n * BLOCK, (n + 1) * BLOCK
        grad_scores = ready
        if hi < length:
            ready = score_grads(n + 1)
        dq_ref[lo:hi, :] = (scale * dot_nn(keys[:, :hi], grad_scores)).T.astype(BF)
        dv = dot_nn(probs_ref[starts[n] : starts[n] + hi, :], grad_all[lo:hi])
        dk = dot_nn(grad_scores, q_ref[lo:hi, :])
        if lo:
            acc_k[:lo, :] += dk[:lo]
            acc_v[:lo, :] += dv[:lo]
        acc_k[lo:hi, :] = dk[lo:]
        acc_v[lo:hi, :] = dv[lo:]
    dk_ref[...] = (scale * acc_k[...]).astype(BF)
    dv_ref[...] = acc_v[...].astype(BF)


def attention(probs, mixed, grad_attn, query, key, value):
    tokens, cols = query.shape
    length = tokens // SEQS
    owners, _, part, _ = grad_attn.shape
    item = pl.BlockSpec((length, HD), lambda s, h: (s, h))
    return kernel_call(
        attention_kernel,
        out_shape=[jax.ShapeDtypeStruct(query.shape, BF)] * 3,
        grid=(SEQS, cols // HD),
        in_specs=[
            pl.BlockSpec((None, None) + probs.shape[2:], lambda s, h: (s, h, 0, 0)),
            item,
            pl.BlockSpec((owners // SEQS, None, part, HD), lambda s, h: (s, h, 0, 0)),
            item,
            item,
            item,
        ],
        out_specs=[item] * 3,
        scratch_shapes=[pltpu.VMEM((length, HD), F32), pltpu.VMEM((length, HD), F32)],
        vmem=24,
        free=(2,),
        name="attention",
    )(probs, mixed, grad_attn, query, key, value)


def exchange(rows, experts):
    total = rows.shape[1]
    moved = lax.all_to_all(
        rows.reshape(experts, SLOTS, total),
        ("group", "inner"),
        split_axis=0,
        concat_axis=0,
        tiled=True,
    )
    return moved.reshape(experts * SLOTS, total)


def local(
    grad_out,
    hidden_in,
    norm_gain,
    expert_ids,
    gate_weights,
    gate_proj,
    up_proj,
    down_proj,
    out_proj,
    query_rows,
    key_rows,
    value_rows,
):
    groups = lax.axis_size("group")
    owners = lax.axis_size("inner")
    experts = groups * owners
    gain = norm_gain.reshape(1, -1)
    tokens, width = grad_out.shape
    piece = out_proj.shape[0] // groups
    ids = expert_ids.T
    own_proj = own_rows(lax.axis_index("group").reshape(1), out_proj, groups)
    own_proj, ids, grad_now, hidden_now = lax.optimization_barrier(
        (own_proj, ids, grad_out, hidden_in)
    )
    proj = lax.all_gather(own_proj, ("group", "inner"), axis=0, tiled=False)
    outgoing = dispatch(ids, grad_now, hidden_now, gain, experts)
    arrived = exchange(outgoing, experts)
    answers, own_scores = expert_backward(arrived, gate_proj[0], up_proj[0], down_proj[0])
    all_scores = lax.all_gather(own_scores, ("group", "inner"), axis=0, tiled=True)
    answers, ids_late, query = lax.optimization_barrier((answers, ids, query_rows))
    back = exchange(answers, experts)
    probs, mixed = attention_probs(query, key_rows, value_rows)
    first, late = plan(ids_late, gate_weights.T, experts)
    back, probs, mixed, first, late = lax.optimization_barrier((back, probs, mixed, first, late))
    grad_hidden, grad_attn = combine(
        first, late, grad_out, hidden_in, gain, back, proj.reshape(groups, owners, piece, width)
    )
    heads = grad_attn.shape[1]
    grad_attn, all_scores = lax.optimization_barrier((grad_attn, all_scores))
    grad_gate = scores(lax.axis_index(("group", "inner")).reshape(1), ids, all_scores).T
    grad_attn = lax.all_to_all(
        grad_attn.reshape(owners, heads * tokens, HD),
        "inner",
        split_axis=0,
        concat_axis=0,
        tiled=True,
    )
    grad_attn, grad_gate = lax.optimization_barrier((grad_attn, grad_gate))
    grad_q, grad_k, grad_v = attention(
        probs,
        mixed,
        grad_attn.reshape(owners, heads, tokens, HD),
        query_rows,
        key_rows,
        value_rows,
    )
    return (grad_hidden, grad_gate, grad_q, grad_k, grad_v)


def solution(mesh):
    rows = P(("group", "inner"), None)
    stack = P(("group", "inner"), None, None)
    heads = P("group", "inner")
    return jax.shard_map(
        local,
        mesh=mesh,
        in_specs=(
            rows,
            rows,
            P(),
            rows,
            rows,
            stack,
            stack,
            stack,
            P("inner", None),
            heads,
            heads,
            heads,
        ),
        out_specs=(rows, rows, heads, heads, heads),
        check_vma=False,
    )
```

```python
import functools

import jax
import jax.numpy as jnp
from jax import lax
from jax.experimental import pallas as pl
from jax.experimental.pallas import tpu as pltpu
from jax.sharding import PartitionSpec as P

HD = 128
SEQS = 2
SLOTS = 8
EXTRA = 2
PARTS = 4
LANES = 128
BF = jnp.bfloat16
F32 = jnp.float32


def dot_nn(left, right):
    return lax.dot_general(left, right, (((1,), (0,)), ((), ())), preferred_element_type=F32)


def dot_nt(left, right):
    return lax.dot_general(left, right, (((1,), (1,)), ((), ())), preferred_element_type=F32)


def dot_tn(left, right):
    return lax.dot_general(left, right, (((0,), (0,)), ((), ())), preferred_element_type=F32)


HELD = pl.BlockSpec(memory_space=pltpu.VMEM)
RAW = pl.BlockSpec(memory_space=pl.ANY)


def kernel_call(kernel, out_shape, vmem, space=pltpu.HBM, free=(), **fields):
    outs = out_shape
    if space is not None:
        outs = jax.tree.map(lambda out: space(out.shape, out.dtype), out_shape)
    call = pl.pallas_call(
        kernel,
        out_shape=outs,
        compiler_params=pltpu.CompilerParams(vmem_limit_bytes=vmem << 20),
        **fields,
    )
    pin = lambda arg: pltpu.with_memory_space_constraint(arg, pltpu.HBM)
    return lambda *args: call(*[arg if n in free else pin(arg) for n, arg in enumerate(args)])


def whole(shape):
    return pl.BlockSpec(shape, lambda i: (0,) * len(shape))


def iota(shape, dim):
    return lax.broadcasted_iota(jnp.int32, shape, dim)


def routing(ids, experts):
    top, tokens = ids.shape
    row = iota((experts, tokens), 0)
    member = jnp.zeros((experts, tokens), F32)
    for k in range(top):
        member = member + jnp.where(ids[k : k + 1, :] == row, 1.0, 0.0)
    earlier = jnp.where(iota((tokens, tokens), 0) < iota((tokens, tokens), 1), 1.0, 0.0).astype(BF)
    slot = dot_nn(member.astype(BF), earlier)
    return jnp.where(member > 0.5, slot, -1.0)


def per_row(by_expert):
    experts, width = by_expert.shape
    return jnp.broadcast_to(by_expert[:, None, :], (experts, SLOTS, width)).reshape(
        experts * SLOTS, width
    )


def own_rows_kernel(place_ref, proj_ref, own_ref):
    own_ref[...] = proj_ref[...]


def own_rows(place, proj, pieces):
    block = (proj.shape[0] // pieces, proj.shape[1])
    return kernel_call(
        own_rows_kernel,
        out_shape=jax.ShapeDtypeStruct(block, BF),
        grid_spec=pltpu.PrefetchScalarGridSpec(
            num_scalar_prefetch=1,
            grid=(1,),
            in_specs=[pl.BlockSpec(block, lambda i, place: (place[0], 0))],
            out_specs=pl.BlockSpec(block, lambda i, place: (0, 0)),
        ),
        vmem=16,
        free=(0,),
        name="own_rows",
    )(place, proj)


def dispatch_kernel(ids_ref, grad_ref, hid_ref, gain_ref, out_ref, rows_ref, parts_ref, slot_ref):
    tokens, width = grad_ref.shape
    experts = slot_ref.shape[0]
    step = pl.program_id(0)
    block_experts = out_ref.shape[0] // SLOTS
    piece = 2 * width // PARTS

    @pl.when(step == 0)
    def _():
        hid = hid_ref[...].astype(F32)
        inv_rms = lax.rsqrt(jnp.mean(hid * hid, axis=1, keepdims=True) + 1e-06)
        normed = (hid * inv_rms * gain_ref[...]).astype(BF)
        grad = grad_ref[...]
        rows_ref[:, :width] = grad
        rows_ref[:, width:] = normed
        half = PARTS // 2
        for part in range(half):
            parts_ref[part * tokens : (part + 1) * tokens, :] = grad[
                :, part * piece : (part + 1) * piece
            ]
            parts_ref[(half + part) * tokens : (half + part + 1) * tokens, :] = normed[
                :, part * piece : (part + 1) * piece
            ]
        slot_ref[...] = routing(ids_ref[...], experts)

    start = pl.multiple_of(step * block_experts, block_experts)
    slot = per_row(slot_ref[pl.ds(start, block_experts), :])
    place = iota(slot.shape, 0) & (SLOTS - 1)
    pick = jnp.where(slot == place.astype(F32), 1.0, 0.0).astype(BF)
    chunk = 1024
    for col in range(0, 2 * width, chunk):
        out_ref[:, col : col + chunk] = dot_nn(pick, rows_ref[:, col : col + chunk]).astype(BF)
    late = slot == (SLOTS + (place >> 2)).astype(F32)
    pick_late = jnp.concatenate(
        [
            jnp.where(late & ((place & (PARTS - 1)) == part), 1.0, 0.0).astype(BF)
            for part in range(PARTS)
        ],
        axis=1,
    )
    out_ref[:, 2 * width :] = dot_nn(pick_late, parts_ref[...]).astype(BF)


def dispatch(ids, grad_out, hidden_in, gain, experts):
    tokens, width = grad_out.shape
    total = 2 * width + 2 * width // PARTS
    steps = 4
    rows = experts * SLOTS
    return kernel_call(
        dispatch_kernel,
        out_shape=jax.ShapeDtypeStruct((rows, total), BF),
        grid=(steps,),
        in_specs=[
            whole(ids.shape),
            whole(grad_out.shape),
            whole(hidden_in.shape),
            whole(gain.shape),
        ],
        out_specs=pl.BlockSpec((rows // steps, total), lambda i: (i, 0)),
        scratch_shapes=[
            pltpu.VMEM((tokens, 2 * width), BF),
            pltpu.VMEM((PARTS * tokens, 2 * width // PARTS), BF),
            pltpu.VMEM((experts, tokens), F32),
        ],
        vmem=16,
        space=None,
        name="dispatch",
    )(ids, grad_out, hidden_in, gain)


def expert_kernel(
    rows_ref, gate_ref, up_ref, down_ref, out_hbm, late_ref, act_ref, out_ref, out_sems
):
    width, hidden = gate_ref.shape
    rows = rows_ref.shape[0]
    group = rows // 2
    late = group // SLOTS * EXTRA
    quarter = width // PARTS
    chunk = 256

    def backward(norm, grad, acts):
        gate_pre = dot_nn(norm(), gate_ref[...])
        up_pre = dot_nn(norm(), up_ref[...])
        score = None
        for col in range(0, hidden, chunk):
            cols = slice(col, col + chunk)
            grad_hid = dot_nt(grad(), down_ref[cols, :])
            gate_part = gate_pre[:, cols]
            sigma = jax.nn.sigmoid(gate_part)
            act = gate_part * sigma
            slope = sigma * (1.0 + gate_part * (1.0 - sigma))
            grad_up = grad_hid * up_pre[:, cols]
            partial = jnp.sum(grad_up * act, axis=1, keepdims=True)
            score = partial if score is None else score + partial
            acts[:, cols] = (grad_up * slope).astype(BF)
            acts[:, hidden + col : hidden + col + chunk] = (grad_hid * act).astype(BF)
        return score

    def pair(acts, cols):
        total = dot_nt(acts[:, :hidden], gate_ref[cols, :])
        return (total + dot_nt(acts[:, hidden:], up_ref[cols, :])).astype(BF)

    sent = []

    def send(lo, height, first, last):
        at = (slice(lo, lo + height), slice(first, last))
        copy = pltpu.make_async_copy(out_ref.at[at], out_hbm.at[at], out_sems.at[len(sent)])
        copy.start()
        sent.append(copy)

    main_scores = []
    for index in range(2):
        at = slice(index * group, (index + 1) * group)
        acts = act_ref.at[at]
        main_scores.append(
            backward(lambda: rows_ref[at, width : 2 * width], lambda: rows_ref[at, :width], acts)
        )
        for col in range(0, width, quarter):
            cols = slice(col, col + quarter)
            out_ref[at, cols] = pair(acts, cols)
        send(index * group, group, 0, width)

    half = group // 2
    few = half // SLOTS * EXTRA
    order = iota((half, half), 0)
    source = (order % few) * PARTS + order // few
    gather = jnp.where(iota((half, half), 1) == source, 1.0, 0.0).astype(BF)
    for block in range(rows // half):
        moved = dot_nn(gather, rows_ref[block * half : (block + 1) * half, 2 * width :]).astype(BF)
        for part in range(PARTS):
            late_ref[block * few : (block + 1) * few, part * 2 * quarter : (part + 1) * 2 * quarter] = (
                moved[part * few : (part + 1) * few]
            )
    acts = act_ref.at[rows:]
    late_score = backward(
        lambda: late_ref[:, width : 2 * width], lambda: late_ref[:, :width], acts
    )
    ends = [pair(acts, slice(col, col + quarter)) for col in range(0, width, quarter)]
    order = iota((half, half), 1)
    scatter = jnp.where(
        iota((half, half), 0) == (order % few) * PARTS + order // few, 1.0, 0.0
    ).astype(BF)
    spread = jnp.where((iota((half, few), 0) >> 2) == iota((half, few), 1), 1.0, 0.0).astype(BF)
    lane = iota((half, LANES), 1)
    for block in range(rows // half):
        at = slice(block * half, (block + 1) * half)
        own = slice(block * few, (block + 1) * few)
        stacked = jnp.concatenate([end[own] for end in ends], axis=0)
        out_ref[at, width : width + quarter] = dot_nn(scatter, stacked).astype(BF)
        spread_score = dot_nn(spread, jnp.broadcast_to(late_score[own], (few, LANES)).astype(BF))
        start = (block % 2) * half
        main_score = main_scores[block // 2][start : start + half]
        out_ref[at, width + quarter :] = jnp.where(
            lane == 0, main_score, jnp.where(lane == 1, spread_score, 0.0)
        ).astype(BF)
    send(0, rows, width, width + quarter + LANES)
    for copy in sent:
        copy.wait()


def expert_backward(arrived, gate_mat, up_mat, down_mat):
    rows = arrived.shape[0]
    width, hidden = gate_mat.shape
    late = rows // SLOTS * EXTRA
    out_shape = (rows, width + width // PARTS + LANES)
    return kernel_call(
        expert_kernel,
        out_shape=jax.ShapeDtypeStruct(out_shape, BF),
        in_specs=[HELD] * 4,
        out_specs=RAW,
        scratch_shapes=[
            pltpu.VMEM((late, 2 * width), BF),
            pltpu.VMEM((rows + late, 2 * hidden), BF),
            pltpu.VMEM(out_shape, BF),
            pltpu.SemaphoreType.DMA((3,)),
        ],
        vmem=24,
        free=(0, 1, 2, 3),
        name="expert",
    )(arrived, gate_mat, up_mat, down_mat)


def placed(ids, rows):
    experts = rows // SLOTS
    slot = per_row(routing(ids, experts))
    place = iota(slot.shape, 0) & (SLOTS - 1)
    return slot == place.astype(F32), slot == (SLOTS + (place >> 2)).astype(F32), place


def plan_kernel(ids_ref, weight_ref, first_ref, late_ref):
    ids = ids_ref[...]
    weights = weight_ref[...]
    top, tokens = ids.shape
    rows = first_ref.shape[1]
    experts = rows // SLOTS
    row = iota((experts, tokens), 0)
    weight = jnp.zeros((experts, tokens), F32)
    for k in range(top):
        weight = weight + jnp.where(ids[k : k + 1, :] == row, weights[k : k + 1, :], 0.0)
    weight = per_row(weight)
    first, late, place = placed(ids, rows)
    high = weight.astype(BF).astype(F32)
    for n, value in enumerate((high, weight - high)):
        first_ref[n * tokens : (n + 1) * tokens, :] = jnp.where(first, value, 0.0).T.astype(BF)
        for part in range(PARTS):
            start = (2 * part + n) * tokens
            hit = late & ((place & (PARTS - 1)) == part)
            late_ref[start : start + tokens, :] = jnp.where(hit, value, 0.0).T.astype(BF)


def plan(ids, weights, experts):
    tokens = ids.shape[1]
    rows = experts * SLOTS
    return kernel_call(
        plan_kernel,
        out_shape=(
            jax.ShapeDtypeStruct((2 * tokens, rows), BF),
            jax.ShapeDtypeStruct((2 * PARTS * tokens, rows), BF),
        ),
        space=pltpu.VMEM,
        vmem=16,
        name="plan",
    )(ids, weights)


def combine_kernel(
    first_ref,
    late_hbm,
    grad_ref,
    hid_ref,
    gain_ref,
    back_hbm,
    proj_hbm,
    out_ref,
    attn_ref,
    back_ref,
    proj_ref,
    late_ref,
    sems,
):
    tokens, width = grad_ref.shape
    quarter = width // PARTS
    pieces, owners, piece, _ = proj_ref.shape
    group = owners // 8
    heads = attn_ref.shape[1]

    def fetch(source, target, n):
        copy = pltpu.make_async_copy(source, target, sems.at[n])
        copy.start()
        return copy

    late_in = fetch(late_hbm, late_ref, PARTS + 9)
    backs = []
    for n, part in enumerate((PARTS,) + tuple(range(PARTS))):
        at = (slice(None), slice(part * quarter, (part + 1) * quarter))
        backs.append(fetch(back_hbm.at[at], back_ref.at[at], n))
    def proj_copy(n):
        at = (slice(None), pl.ds(n * group, group))
        return pltpu.make_async_copy(proj_hbm.at[at], proj_ref.at[at], sems.at[len(backs) + n])

    for n in range(8):
        proj_copy(n).start()

    hid = hid_ref[...].astype(F32)
    inv_rms = lax.rsqrt(jnp.mean(hid * hid, axis=1, keepdims=True) + 1e-06)
    late_in.wait()
    backs[0].wait()
    late = dot_nn(late_ref[...], back_ref[:, width:])
    total = jnp.zeros((tokens, 1), F32)
    parts = []
    for part in range(PARTS):
        cols = slice(part * quarter, (part + 1) * quarter)
        backs[1 + part].wait()
        moe = dot_nn(first_ref[...], back_ref[:, cols])
        begin = 2 * part * tokens
        moe = (moe[:tokens] + moe[tokens:]) + (
            late[begin : begin + tokens] + late[begin + tokens : begin + 2 * tokens]
        )
        scaled = moe * gain_ref[:, cols]
        parts.append(scaled)
        total = total + jnp.sum(scaled * (hid[:, cols] * inv_rms), axis=1, keepdims=True)
    inner_mean = total * (1.0 / width)
    for part in range(PARTS):
        cols = slice(part * quarter, (part + 1) * quarter)
        change = parts[part] - hid[:, cols] * inv_rms * inner_mean
        out_ref[:, cols] = (grad_ref[:, cols].astype(F32) + inv_rms * change).astype(BF)

    def project(n, carry):
        proj_copy(n).wait()
        for index in range(group):
            owner = n * group + index
            proj = proj_ref[:, owner].reshape(pieces * piece, width)
            grad = dot_nt(out_ref[...], proj).astype(BF)
            for head in range(heads):
                attn_ref[owner, head] = grad[:, head * HD : (head + 1) * HD]
        return carry

    lax.fori_loop(0, 8, project, 0)


def combine(first, late, grad_out, hidden_in, gain, back, proj):
    tokens, width = grad_out.shape
    pieces, owners, piece, _ = proj.shape
    heads = pieces * piece // HD
    return kernel_call(
        combine_kernel,
        out_shape=(
            jax.ShapeDtypeStruct(grad_out.shape, BF),
            jax.ShapeDtypeStruct((owners, heads, tokens, HD), BF),
        ),
        in_specs=[HELD, RAW] + [HELD] * 3 + [RAW] * 2,
        out_specs=(HELD, HELD),
        scratch_shapes=[
            pltpu.VMEM((back.shape[0], width + width // PARTS), BF),
            pltpu.VMEM(proj.shape, BF),
            pltpu.VMEM(late.shape, BF),
            pltpu.SemaphoreType.DMA((PARTS + 10,)),
        ],
        vmem=50,
        space=None,
        free=(0, 1, 2, 3, 4),
        name="combine",
    )(first, late, grad_out, hidden_in, gain, back, proj)


def score_kernel(ids_ref, score_ref, gate_ref):
    ids = ids_ref[...]
    top, tokens = ids.shape
    rows = score_ref.shape[0]
    experts = rows // SLOTS
    score = score_ref[...].astype(F32)
    first, late, place = placed(ids, rows)
    got = jnp.where(first, score[:, 0:1], 0.0) + jnp.where(
        late & ((place & (PARTS - 1)) == 0), score[:, 1:2], 0.0
    )
    by_expert = jnp.sum(got.reshape(experts, SLOTS, tokens), axis=1)
    row = iota((experts, tokens), 0)
    gates = [
        jnp.sum(jnp.where(ids[k : k + 1, :] == row, by_expert, 0.0), axis=0, keepdims=True)
        for k in range(top)
    ]
    gate_ref[...] = jnp.concatenate(gates, axis=0).astype(BF)


def scores(ids, back):
    rows, total = back.shape
    return kernel_call(
        score_kernel,
        out_shape=jax.ShapeDtypeStruct(ids.shape, BF),
        grid=(1,),
        in_specs=[
            whole(ids.shape),
            pl.BlockSpec((rows, LANES), lambda i: (0, total // LANES - 1)),
        ],
        out_specs=whole(ids.shape),
        vmem=16,
        name="scores",
    )(ids, back)


BLOCK = 256


def probs_kernel(q_ref, k_ref, v_ref, out_ref, mixed_ref):
    length = q_ref.shape[0]
    scale = HD ** (-0.5)
    start = 0
    for lo in range(0, length, BLOCK):
        hi = lo + BLOCK
        scores = dot_nt(k_ref[:hi, :], q_ref[lo:hi, :])
        corner = jnp.where(
            iota((BLOCK, BLOCK), 0) <= iota((BLOCK, BLOCK), 1), scores[lo:], -jnp.inf
        )
        scores = jnp.concatenate([scores[:lo], corner], axis=0) if lo else corner
        peak = jnp.max(scores, axis=0, keepdims=True)
        exp_scores = jnp.exp((scores - peak) * scale)
        total = jnp.sum(exp_scores, axis=0, keepdims=True)
        probs = (exp_scores * (1.0 / total)).astype(BF)
        out_ref[start : start + hi, :] = probs
        mixed_ref[lo:hi, :] = dot_tn(probs, v_ref[:hi, :])
        start += hi


def packed_rows(length):
    return sum(range(BLOCK, length + 1, BLOCK))


def attention_probs(query, key, value):
    tokens, cols = query.shape
    length = tokens // SEQS
    heads = cols // HD
    item = pl.BlockSpec((length, HD), lambda s, h: (s, h))
    rows = packed_rows(length)
    return kernel_call(
        probs_kernel,
        out_shape=(
            jax.ShapeDtypeStruct((SEQS, heads, rows, BLOCK), BF),
            jax.ShapeDtypeStruct(query.shape, F32),
        ),
        grid=(SEQS, heads),
        in_specs=[item] * 3,
        out_specs=(pl.BlockSpec((None, None, rows, BLOCK), lambda s, h: (s, h, 0, 0)), item),
        vmem=20,
        name="probs",
    )(query, key, value)


def attention_kernel(
    probs_ref, mixed_ref, grad_ref, q_ref, k_ref, v_ref, dq_ref, dk_ref, dv_ref, acc_k, acc_v
):
    length = q_ref.shape[0]
    scale = HD ** (-0.5)
    grad_all = grad_ref[...].reshape(length, HD)
    less = -jnp.sum(grad_all.astype(F32) * mixed_ref[...], axis=1, keepdims=True)
    high = less.astype(BF).astype(F32)
    mid = (less - high).astype(BF).astype(F32)
    low = less - high - mid
    lane = iota((length, HD), 1)
    extra = jnp.where(lane == 0, high, jnp.where(lane == 1, mid, jnp.where(lane == 2, low, 0.0)))
    grad_less = jnp.concatenate([grad_all, extra.astype(BF)], axis=1)
    ones = jnp.where(lane < 3, 1.0, 0.0).astype(BF)
    values = jnp.concatenate([v_ref[...], ones], axis=1)
    keys = k_ref[...].T
    starts = [BLOCK * n * (n + 1) // 2 for n in range(length // BLOCK)]

    def score_grads(n):
        hi = (n + 1) * BLOCK
        shifted = dot_nt(values[:hi], grad_less[hi - BLOCK : hi])
        probs = probs_ref[starts[n] : starts[n] + hi, :]
        return (probs.astype(F32) * shifted).astype(BF)

    ready = score_grads(0)
    for n in range(length // BLOCK):
        lo, hi = n * BLOCK, (n + 1) * BLOCK
        grad_scores = ready
        if hi < length:
            ready = score_grads(n + 1)
        dq_ref[lo:hi, :] = (scale * dot_nn(keys[:, :hi], grad_scores)).T.astype(BF)
        dv = dot_nn(probs_ref[starts[n] : starts[n] + hi, :], grad_all[lo:hi])
        dk = dot_nn(grad_scores, q_ref[lo:hi, :])
        if lo:
            acc_k[:lo, :] += dk[:lo]
            acc_v[:lo, :] += dv[:lo]
        acc_k[lo:hi, :] = dk[lo:]
        acc_v[lo:hi, :] = dv[lo:]
    dk_ref[...] = (scale * acc_k[...]).astype(BF)
    dv_ref[...] = acc_v[...].astype(BF)


def attention(probs, mixed, grad_attn, query, key, value):
    tokens, cols = query.shape
    length = tokens // SEQS
    owners, _, part, _ = grad_attn.shape
    item = pl.BlockSpec((length, HD), lambda s, h: (s, h))
    return kernel_call(
        attention_kernel,
        out_shape=[jax.ShapeDtypeStruct(query.shape, BF)] * 3,
        grid=(SEQS, cols // HD),
        in_specs=[
            pl.BlockSpec((None, None) + probs.shape[2:], lambda s, h: (s, h, 0, 0)),
            item,
            pl.BlockSpec((owners // SEQS, None, part, HD), lambda s, h: (s, h, 0, 0)),
            item,
            item,
            item,
        ],
        out_specs=[item] * 3,
        scratch_shapes=[pltpu.VMEM((length, HD), F32), pltpu.VMEM((length, HD), F32)],
        vmem=24,
        free=(2,),
        name="attention",
    )(probs, mixed, grad_attn, query, key, value)


def exchange(rows, experts):
    total = rows.shape[1]
    moved = lax.all_to_all(
        rows.reshape(experts, SLOTS, total),
        ("group", "inner"),
        split_axis=0,
        concat_axis=0,
        tiled=True,
    )
    return moved.reshape(experts * SLOTS, total)


def local(
    grad_out,
    hidden_in,
    norm_gain,
    expert_ids,
    gate_weights,
    gate_proj,
    up_proj,
    down_proj,
    out_proj,
    query_rows,
    key_rows,
    value_rows,
):
    groups = lax.axis_size("group")
    owners = lax.axis_size("inner")
    experts = groups * owners
    gain = norm_gain.reshape(1, -1)
    tokens, width = grad_out.shape
    piece = out_proj.shape[0] // groups
    ids = expert_ids.T
    own_proj = own_rows(lax.axis_index("group").reshape(1), out_proj, groups)
    own_proj, ids, grad_now, hidden_now = lax.optimization_barrier(
        (own_proj, ids, grad_out, hidden_in)
    )
    proj = lax.all_gather(own_proj, ("group", "inner"), axis=0, tiled=False)
    outgoing = dispatch(ids, grad_now, hidden_now, gain, experts)
    arrived = exchange(outgoing, experts)
    answers = expert_backward(arrived, gate_proj[0], up_proj[0], down_proj[0])
    answers, ids_late, query = lax.optimization_barrier((answers, ids, query_rows))
    back = exchange(answers, experts)
    probs, mixed = attention_probs(query, key_rows, value_rows)
    first, late = plan(ids_late, gate_weights.T, experts)
    back, probs, mixed, first, late = lax.optimization_barrier((back, probs, mixed, first, late))
    grad_hidden, grad_attn = combine(
        first, late, grad_out, hidden_in, gain, back, proj.reshape(groups, owners, piece, width)
    )
    heads = grad_attn.shape[1]
    grad_attn, back = lax.optimization_barrier((grad_attn, back))
    grad_gate = scores(ids, back).T
    grad_attn = lax.all_to_all(
        grad_attn.reshape(owners, heads * tokens, HD),
        "inner",
        split_axis=0,
        concat_axis=0,
        tiled=True,
    )
    grad_attn, grad_gate = lax.optimization_barrier((grad_attn, grad_gate))
    grad_q, grad_k, grad_v = attention(
        probs,
        mixed,
        grad_attn.reshape(owners, heads, tokens, HD),
        query_rows,
        key_rows,
        value_rows,
    )
    return (grad_hidden, grad_gate, grad_q, grad_k, grad_v)


def solution(mesh):
    rows = P(("group", "inner"), None)
    stack = P(("group", "inner"), None, None)
    heads = P("group", "inner")
    return jax.shard_map(
        local,
        mesh=mesh,
        in_specs=(
            rows,
            rows,
            P(),
            rows,
            rows,
            stack,
            stack,
            stack,
            P("inner", None),
            heads,
            heads,
            heads,
        ),
        out_specs=(rows, rows, heads, heads, heads),
        check_vma=False,
    )
```
